32 devices in a mesh: seq: 4 (over y, x), fsdp: 8 (over z, core).
Axes of the slice: x: 2, y: 2, z: 4, core: 2. Of those that a mesh axis runs over, the one named last changes fastest.
Arguments:
- layer_in: float32 [2, 4, 1024, 2048], P(None, 'seq', 'fsdp'), may hold values from -6 to 6
- doc_ids: int32 [2, 4, 1024], P(None, 'seq'), may hold values from 0 to 3, as said below
- out_grad: float32 [2, 4, 1024, 2048], P(None, 'seq', 'fsdp'), may hold values from -6 to 6
- query_weight: float32 [2048, 2048], P(('seq', 'fsdp')), may hold values from -0.125 to 0.125
- query_bias: float32 [2048], P(('seq', 'fsdp')), may hold values from -3 to 3
- key_weight: float32 [2048, 2048], P(('seq', 'fsdp')), may hold values from -0.1875 to 0.1875
- value_weight: float32 [2048, 2048], P(('seq', 'fsdp')), may hold values from -0.125 to 0.125
- value_bias: float32 [2048], P(('seq', 'fsdp')), may hold values from -2 to 2
- output_weight: float32 [2048, 2048], P(('seq', 'fsdp')), may hold values from -2 to 2
- output_bias: float32 [2048], P(('seq', 'fsdp')), may hold values from -3 to 3
- first_gain: float32 [2048], P(('seq', 'fsdp')), may hold values from 0.25 to 1.75
- first_shift: float32 [2048], P(('seq', 'fsdp')), may hold values from -2 to 2
- up_weight: float32 [2048, 8192], P(('seq', 'fsdp')), may hold values from -0.125 to 0.125
- up_bias: float32 [8192], P(('seq', 'fsdp')), may hold values from -3 to 3
- down_weight: float32 [8192, 2048], P(('seq', 'fsdp')), may hold values from -0.0625 to 0.0625
- down_bias: float32 [2048], P(('seq', 'fsdp')), may hold values from -3 to 3
- second_gain: float32 [2048], P(('seq', 'fsdp')), may hold values from 0.25 to 1.75
- second_shift: float32 [2048], P(('seq', 'fsdp')), may hold values from -2 to 2
Outputs:
- layer_out: float32 [2, 4, 1024, 2048], P(None, 'seq', 'fsdp')
- input_grad: float32 [2, 4, 1024, 2048], P(None, 'seq', 'fsdp')
- query_weight_grad: float32 [2048, 2048], P(('seq', 'fsdp'))
- query_bias_grad: float32 [2048], P(('seq', 'fsdp'))
- key_weight_grad: float32 [2048, 2048], P(('seq', 'fsdp'))
- value_weight_grad: float32 [2048, 2048], P(('seq', 'fsdp'))
- value_bias_grad: float32 [2048], P(('seq', 'fsdp'))
- output_weight_grad: float32 [2048, 2048], P(('seq', 'fsdp'))
- output_bias_grad: float32 [2048], P(('seq', 'fsdp'))
- first_gain_grad: float32 [2048], P(('seq', 'fsdp'))
- first_shift_grad: float32 [2048], P(('seq', 'fsdp'))
- up_weight_grad: float32 [2048, 8192], P(('seq', 'fsdp'))
- up_bias_grad: float32 [8192], P(('seq', 'fsdp'))
- down_weight_grad: float32 [8192, 2048], P(('seq', 'fsdp'))
- down_bias_grad: float32 [2048], P(('seq', 'fsdp'))
- second_gain_grad: float32 [2048], P(('seq', 'fsdp'))
- second_shift_grad: float32 [2048], P(('seq', 'fsdp'))
The draws below stay inside these ranges and needn't reach their ends.
Inputs may be any that keep to these rules, and one draw needn't show every extreme that they name: `doc_ids`: within a sequence the document numbers never fall, every one of the 4 numbers occurs, and each document holds 102 to 718 tokens; in every draw some sequence has a document of exactly 718 tokens.
All inputs are finite; a program needn't handle non-finite values.
Results may differ from the reference program's by a relative error of at most 0.015.
The reference program's roundings to bfloat16 on the way count: a program that leaves them out, or rounds other values in their place, can miss the bound.
Values may be sent and summed in bfloat16 or wider, within the bound.
No kernel may reach another device: no remote copies, remote signals or barrier semaphores. Data moves between devices by JAX's collectives and lax.ppermute only.
A program may use at most 512 MiB of HBM per device.

```python
import jax
import jax.numpy as jnp
from jax import lax

D = 2048
H = 16
DH = 128
FF = 8192
MB = 2
DOCS = 4
L = 1024
SEQS = 4
DOC_LEAST = 102


def draw_doc_ids(key, part):
    row_count = MB * SEQS
    spare = L - DOCS * DOC_LEAST
    cut_key = jax.random.fold_in(key, 11)
    big_key = jax.random.fold_in(key, 23)
    cuts = jnp.sort(jax.random.randint(cut_key, (row_count, DOCS - 1), 0, spare + 1), axis=1)
    edges = jnp.concatenate([jnp.zeros((row_count, 1), jnp.int32), cuts.astype(jnp.int32), jnp.full((row_count, 1), spare, jnp.int32)], axis=1)
    extras = edges[:, 1:] - edges[:, :-1]
    chosen = jax.random.randint(big_key, (), 0, DOCS)
    single = jnp.where(jnp.arange(DOCS) == chosen, spare, 0).astype(jnp.int32)
    first_row = (jnp.arange(row_count) == 0)[:, None]
    extras = jnp.where(first_row, single[None, :], extras)
    lengths = extras + DOC_LEAST
    ends = jnp.cumsum(lengths, axis=1)[:, :DOCS - 1]
    positions = jnp.arange(L, dtype=jnp.int32)
    numbers = jnp.sum((positions[None, :, None] >= ends[:, None, :]).astype(jnp.int32), axis=-1)
    return numbers.reshape(MB, SEQS, L).astype(jnp.int32)


def shard_levels(own_key, extent, shards, least, largest):
    loudness = 1.0
    for axis_at, shards_of in shards:
        steps = jax.random.uniform(jax.random.fold_in(jax.random.fold_in(own_key, 6), axis_at), (shards_of,), jnp.float32, least / len(shards), largest / len(shards))
        loudness = loudness * jnp.repeat(jnp.exp(steps), extent[axis_at] // shards_of).reshape((-1,) + (1,) * (len(extent) - 1 - axis_at))
    return loudness


def bell_draw(own_key, shape, width, reach, split=(), held_as=jnp.bfloat16):
    entries = jax.random.normal(own_key, shape, jnp.float32) * width
    if len(split) > 0:
        entries = shard_levels(own_key, shape, split, -0.22, 0.18) * entries
    return jnp.clip(entries, min=-reach, max=reach).astype(held_as)


def setup_inputs(seed: int = 0) -> dict:
    key_list = jax.random.split(jax.random.key(seed), 19)
    layer_in = bell_draw(key_list[0], (MB, SEQS, L, D), 1.0, 6.0, ((1, 4), (2, 8)), jnp.float32)
    doc_ids = draw_doc_ids(jax.random.fold_in(key_list[18], 71), 0)
    out_grad = bell_draw(key_list[2], (MB, SEQS, L, D), 1.0, 6.0, ((1, 4), (2, 8)), jnp.float32)
    query_weight = bell_draw(key_list[3], (D, D), D ** -0.5, 0.125, ((0, 32),), jnp.float32)
    query_bias = bell_draw(key_list[4], (D,), 0.5, 3.0, ((0, 32),), jnp.float32)
    key_weight = bell_draw(key_list[5], (D, D), (D // 2) ** -0.5, 0.1875, ((0, 32),), jnp.float32)
    value_weight = bell_draw(key_list[6], (D, D), D ** -0.5, 0.125, ((0, 32),), jnp.float32)
    value_bias = bell_draw(key_list[7], (D,), 0.3, 2.0, ((0, 32),), jnp.float32)
    output_weight = bell_draw(key_list[8], (D, D), (max(D // 256, 1)) ** -0.5, 2.0, ((0, 32),), jnp.float32)
    output_bias = bell_draw(key_list[9], (D,), 0.5, 3.0, ((0, 32),), jnp.float32)
    first_gain = jnp.clip(1.0 + 0.15 * jax.random.normal(key_list[10], (D,), jnp.float32), 0.25, 1.75)
    first_shift = bell_draw(key_list[11], (D,), 0.3, 2.0, ((0, 32),), jnp.float32)
    up_weight = bell_draw(key_list[12], (D, FF), D ** -0.5, 0.125, ((0, 32),), jnp.float32)
    up_bias = bell_draw(key_list[13], (FF,), 0.5, 3.0, ((0, 32),), jnp.float32)
    down_weight = bell_draw(key_list[14], (FF, D), FF ** -0.5, 0.0625, ((0, 32),), jnp.float32)
    down_bias = bell_draw(key_list[15], (D,), 0.5, 3.0, ((0, 32),), jnp.float32)
    second_gain = jnp.clip(1.0 + 0.15 * jax.random.normal(key_list[16], (D,), jnp.float32), 0.25, 1.75)
    second_shift = bell_draw(key_list[17], (D,), 0.3, 2.0, ((0, 32),), jnp.float32)
    return {"layer_in": layer_in, "doc_ids": doc_ids, "out_grad": out_grad, "query_weight": query_weight, "query_bias": query_bias, "key_weight": key_weight, "value_weight": value_weight, "value_bias": value_bias, "output_weight": output_weight, "output_bias": output_bias, "first_gain": first_gain, "first_shift": first_shift, "up_weight": up_weight, "up_bias": up_bias, "down_weight": down_weight, "down_bias": down_bias, "second_gain": second_gain, "second_shift": second_shift}


@jax.custom_vjp
def low(v):
    return lax.optimization_barrier(v.astype(jnp.bfloat16)).astype(jnp.float32)

@jax.custom_vjp
def low_back(v):
    return v

def low_keep(v):
    return (low(v), None)

def low_pass(kept, grad):
    return (grad,)

def back_keep(v):
    return (v, None)

def back_low(kept, grad):
    return (low(grad),)
low.defvjp(low_keep, low_pass)
low_back.defvjp(back_keep, back_low)
norm_eps = 1e-06
masked_score = -1e+30

def product(left, right):
    return jnp.dot(left, right, precision=lax.Precision.HIGHEST)

def normalize(summed, gain_vector, shift_vector):
    center = summed - lax.optimization_barrier(jnp.mean(summed, axis=-1, keepdims=True))
    spread = lax.optimization_barrier(jnp.mean(center * center, axis=-1, keepdims=True))
    return center * lax.rsqrt(spread + norm_eps) * gain_vector + shift_vector

def layer(inputs, doc_row, params):
    query_weight, query_bias, key_weight, value_weight, value_bias, output_weight, output_bias, first_gain, first_shift, up_weight, up_bias, down_weight, down_bias, second_gain, second_shift = params
    length = inputs.shape[0]
    rounded_in = low(inputs)
    queries = low(low_back(product(rounded_in, low(query_weight)) + low(query_bias)))
    keys = low(low_back(product(rounded_in, low(key_weight))))
    values = low(low_back(product(rounded_in, low(value_weight)) + low(value_bias)))
    query_heads = queries.reshape(length, H, DH)
    key_heads = keys.reshape(length, H, DH)
    value_heads = values.reshape(length, H, DH)
    scores = jnp.einsum('qhd,khd->hqk', query_heads, key_heads, precision=lax.Precision.HIGHEST) * DH ** (-0.5)
    same_doc = doc_row[:, None] == doc_row[None, :]
    scores = low_back(jnp.where(same_doc[None], scores, masked_score))
    attend = jax.nn.softmax(scores, axis=-1)
    mixed_rows = jnp.einsum('hqk,khd->qhd', low(attend), value_heads, precision=lax.Precision.HIGHEST).reshape(length, D)
    mixed_rows = low(low_back(mixed_rows))
    branch = low_back(product(mixed_rows, low(output_weight)) + low(output_bias))
    hidden = normalize(inputs + branch, low(first_gain), low(first_shift))
    up_rows = low_back(product(low(hidden), low(up_weight)) + low(up_bias))
    active = low(jax.nn.gelu(up_rows, approximate=True))
    down_rows = low_back(product(active, low(down_weight)) + low(down_bias))
    return normalize(hidden + down_rows, low(second_gain), low(second_shift))

def reference(layer_in, doc_ids, out_grad, query_weight, query_bias, key_weight, value_weight, value_bias, output_weight, output_bias, first_gain, first_shift, up_weight, up_bias, down_weight, down_bias, second_gain, second_shift):
    params = (query_weight, query_bias, key_weight, value_weight, value_bias, output_weight, output_bias, first_gain, first_shift, up_weight, up_bias, down_weight, down_bias, second_gain, second_shift)
    flat_in = layer_in.reshape(MB * SEQS, L, D)
    flat_ids = doc_ids.reshape(MB * SEQS, L)
    checked = jax.checkpoint(layer)

    def forward(inputs, weights):
        return lax.map(lambda sequence_pair: checked(sequence_pair[0], sequence_pair[1], weights), (inputs, flat_ids))
    result, pullback = jax.vjp(forward, flat_in, params)
    grad_in, grads = pullback(out_grad.reshape(MB * SEQS, L, D))
    return (result.reshape(MB, SEQS, L, D), grad_in.reshape(MB, SEQS, L, D), grads[0], grads[1], grads[2], grads[3], grads[4], grads[5], grads[6], grads[7], grads[8], grads[9], grads[10], grads[11], grads[12], grads[13], grads[14])
```

```python
import functools

import jax
import jax.numpy as jnp
from jax import lax
from jax.experimental import pallas as pl
from jax.experimental.pallas import tpu as pltpu
from jax.sharding import Mesh
from jax.sharding import PartitionSpec as P

D = 2048
H = 16
DH = 128
MB = 2
CORES = 2

low = jnp.bfloat16
wide = jnp.float32
norm_eps = 1e-06
masked_score = -1e30
score_scale = DH ** (-0.5)
ALL = ("seq", "z", "c")


def normalize_forward(summed, gain_vector, shift_vector):
    center = summed - jnp.mean(summed, axis=-1, keepdims=True)
    inverse = lax.rsqrt(jnp.mean(center * center, axis=-1, keepdims=True) + norm_eps)
    normed = center * inverse
    return (normed * gain_vector + shift_vector, normed, inverse)


def normalize_backward(grad_output, normed, inverse, gain_vector):
    grad_normed = grad_output * gain_vector
    centered = grad_normed - jnp.mean(grad_normed, axis=-1, keepdims=True)
    grad_input = inverse * (
        centered - normed * jnp.mean(grad_normed * normed, axis=-1, keepdims=True)
    )
    return (grad_input, jnp.sum(grad_output * normed, axis=0), jnp.sum(grad_output, axis=0))


def matmul(left, right):
    return jnp.dot(left, right, preferred_element_type=wide)


def transposed(left, right):
    return jnp.einsum("ti,tj->ij", left, right, preferred_element_type=wide)


def against(left, right):
    return jnp.einsum("ti,ji->tj", left, right, preferred_element_type=wide)


def column_sum(matrix):
    return jnp.sum(matrix.astype(wide), axis=0)


def gelu_both(u):
    root = (2.0 / jnp.pi) ** 0.5
    cubic = 0.044715
    square = u * u
    bend = jnp.tanh(root * (u + cubic * u * square))
    half = 0.5 * (1.0 + bend)
    slope = half + 0.5 * u * (1.0 - bend * bend) * (root * (1.0 + 3.0 * cubic * square))
    return u * half, slope


def nt(left, right):
    return lax.dot_general(left, right, (((1,), (1,)), ((), ())), preferred_element_type=wide)


def tn(left, right):
    return lax.dot_general(left, right, (((0,), (0,)), ((), ())), preferred_element_type=wide)


def attend_kernel(rows, q_ref, k_ref, v_ref, row_ref, col_ref, o_ref, total_ref):
    keys = k_ref[...]
    values = v_ref[...]
    cols = col_ref[...]
    for start in range(0, q_ref.shape[0], rows):
        here = pl.ds(start, rows)
        scores = nt(q_ref[here, :], keys) * score_scale
        scores = jnp.where(row_ref[here, :] == cols, scores, masked_score)
        top = jnp.max(scores, axis=-1, keepdims=True)
        raised = jnp.exp(scores - top)
        total = jnp.sum(raised, axis=-1, keepdims=True)
        probs = (raised * (1.0 / total)).astype(low)
        o_ref[here, :] = jnp.dot(probs, values, preferred_element_type=wide).astype(low)
        total_ref[0, here, :] = top + jnp.log(total)


def attend_back_kernel(
    rows, q_ref, k_ref, v_ref, g_ref, total_ref, row_ref, col_ref, dq_ref, dk_ref, dv_ref, ka, va
):
    keys = k_ref[...]
    values = v_ref[...]
    cols = col_ref[...]
    for start in range(0, q_ref.shape[0], rows):
        here = pl.ds(start, rows)
        queries = q_ref[here, :]
        grads = g_ref[here, :]
        scores = nt(queries, keys) * score_scale
        scores = jnp.where(row_ref[here, :] == cols, scores, masked_score)
        probs = jnp.exp(scores - total_ref[0, here, :])
        grad_probs = nt(grads, values)
        row_dot = jnp.sum(probs * grad_probs, axis=-1, keepdims=True)
        grad_scores = (probs * (grad_probs - row_dot)).astype(low)
        dq_ref[here, :] = (
            jnp.dot(grad_scores, keys, preferred_element_type=wide) * score_scale
        ).astype(low)
        dk_part = tn(grad_scores, queries)
        dv_part = tn(probs.astype(low), grads)
        if start == 0:
            ka[...] = dk_part
            va[...] = dv_part
        else:
            ka[...] += dk_part
            va[...] += dv_part
    dk_ref[...] = (ka[...] * score_scale).astype(low)
    dv_ref[...] = va[...].astype(low)


def attend(qkv, row_ids, col_ids, heads):
    length = qkv.shape[0]
    rows = min(256, length)
    block = lambda part: pl.BlockSpec((length, DH), lambda h: (0, part * heads + h))
    return pl.pallas_call(
        functools.partial(attend_kernel, rows),
        grid=(heads,),
        in_specs=[
            block(0),
            block(1),
            block(2),
            pl.BlockSpec((length, 1), lambda h: (0, 0)),
            pl.BlockSpec((1, length), lambda h: (0, 0)),
        ],
        out_specs=[
            pl.BlockSpec((length, DH), lambda h: (0, h)),
            pl.BlockSpec((1, length, 1), lambda h: (h, 0, 0)),
        ],
        out_shape=[
            jax.ShapeDtypeStruct((length, heads * DH), low),
            jax.ShapeDtypeStruct((heads, length, 1), wide),
        ],
        cost_estimate=pl.CostEstimate(
            flops=4 * heads * length * length * DH,
            bytes_accessed=8 * heads * length * DH,
            transcendentals=heads * length * length,
        ),
        compiler_params=pltpu.CompilerParams(vmem_limit_bytes=40 * 2**20),
        name="attend",
    )(qkv, qkv, qkv, row_ids, col_ids)


def attend_back(qkv, grad_mixed, totals, row_ids, col_ids, heads):
    length = qkv.shape[0]
    rows = min(256, length)
    block = lambda part: pl.BlockSpec((length, DH), lambda h: (0, part * heads + h))
    out = pl.BlockSpec((length, DH), lambda h: (0, h))
    shape = jax.ShapeDtypeStruct((length, heads * DH), low)
    return pl.pallas_call(
        functools.partial(attend_back_kernel, rows),
        grid=(heads,),
        in_specs=[
            block(0),
            block(1),
            block(2),
            out,
            pl.BlockSpec((1, length, 1), lambda h: (h, 0, 0)),
            pl.BlockSpec((length, 1), lambda h: (0, 0)),
            pl.BlockSpec((1, length), lambda h: (0, 0)),
        ],
        out_specs=[out, out, out],
        out_shape=[shape, shape, shape],
        scratch_shapes=[pltpu.VMEM((length, DH), wide), pltpu.VMEM((length, DH), wide)],
        cost_estimate=pl.CostEstimate(
            flops=10 * heads * length * length * DH,
            bytes_accessed=16 * heads * length * DH,
            transcendentals=heads * length * length,
        ),
        compiler_params=pltpu.CompilerParams(vmem_limit_bytes=48 * 2**20),
        name="attend_back",
    )(qkv, qkv, qkv, grad_mixed, totals, row_ids, col_ids)


def swap(value, axis, size, bit):
    return lax.ppermute(value, axis, [(i, i ^ bit) for i in range(size)])


def exchange(value, axis, size):
    here = lax.axis_index(axis)
    pick = lambda i: lax.dynamic_index_in_dim(value, i, 0, keepdims=True)
    result = value
    for k in range(1, size):
        came = swap(pick(here ^ k), axis, size, k)
        result = lax.dynamic_update_slice_in_dim(result, came, here ^ k, 0)
    return result


def bits(size):
    step = 1
    while step < size:
        yield step
        step *= 2


def sum_all(value, sizes):
    for axis in ("c", "z", "seq"):
        for bit in bits(sizes[axis]):
            value = value + swap(value, axis, sizes[axis], bit)
    return value


ENDS = [(0, 1), (1, 0), (2, 3), (3, 2)]
MIDDLE = [(1, 2), (2, 1)]
OUTWARD = [(1, 0), (2, 3)]
INWARD = [(0, 1), (3, 2)]


def gather_slots(own, axis, size):
    if size != 4:
        whole = lax.all_gather(own, axis, axis=0)
        return [whole[i] for i in range(size)]
    send = lambda value, pairs: lax.ppermute(value, axis, pairs)
    if axis == "z":
        inner = (lax.axis_index(axis) == 1) | (lax.axis_index(axis) == 2)
        first = send(own, ENDS)
        third_in = send(own, MIDDLE)
        second_in = send(first, MIDDLE)
        second_out = send(third_in, OUTWARD)
        third_out = send(second_in, OUTWARD)
        return [
            own,
            first,
            jnp.where(inner, second_in, second_out),
            jnp.where(inner, third_in, third_out),
        ]
    half = own.shape[0] // 2
    first = swap(own, axis, 4, 1)
    second = swap(own, axis, 4, 2)
    third_top = swap(first[:half], axis, 4, 2)
    third_end = swap(second[half:], axis, 4, 1)
    return [own, first, second, jnp.concatenate([third_top, third_end], axis=0)]


def scatter_slots(parts, axis, size):
    if size != 4:
        return lax.psum_scatter(jnp.stack(parts), axis, scatter_dimension=0, tiled=False).astype(
            wide
        )
    send = lambda value, pairs: lax.ppermute(value, axis, pairs)
    add = lambda a, b: (a.astype(wide) + b.astype(wide)).astype(low)
    own, first, second, third = parts
    if axis == "z":
        second_full = add(second, send(third, INWARD))
        third_full = add(third, send(second, INWARD))
        first_full = add(first, send(second_full, MIDDLE))
        from_middle = send(third_full, MIDDLE)
        from_end = send(first_full, ENDS)
        return own.astype(wide) + from_middle.astype(wide) + from_end.astype(wide)
    half = own.shape[0] // 2
    top = swap(third[:half], axis, 4, 2)
    end = swap(third[half:], axis, 4, 1)
    first_full = jnp.concatenate([add(first[:half], top), first[half:]], axis=0)
    second_full = jnp.concatenate([second[:half], add(second[half:], end)], axis=0)
    from_first = swap(first_full, axis, 4, 1)
    from_second = swap(second_full, axis, 4, 2)
    return own.astype(wide) + from_first.astype(wide) + from_second.astype(wide)


def slot_order(axis, size):
    order = jnp.arange(size)
    return order ^ lax.axis_index(axis) if size == 4 else order


def split_slots(value, size):
    step = value.shape[0] // size
    return [value[i * step : (i + 1) * step] for i in range(size)]


def shards(
    sizes,
    layer_in,
    doc_ids,
    out_grad,
    query_weight,
    query_bias,
    key_weight,
    value_weight,
    value_bias,
    output_weight,
    output_bias,
    first_gain,
    first_shift,
    up_weight,
    up_bias,
    down_weight,
    down_bias,
    second_gain,
    second_shift,
):
    S, Z, C = sizes["seq"], sizes["z"], sizes["c"]
    F = Z * C
    devices = S * F
    s, z, c = (lax.axis_index(a) for a in ALL)
    mine = (s * Z + z) * C + c
    rows = query_weight.shape[0]
    hidden_units = up_weight.shape[1]
    share = hidden_units // devices
    slice_width = hidden_units // S
    heads = H // Z
    tokens = layer_in.shape[2]
    whole_heads = rows * C == DH

    def to_core(value):
        keep = lax.dynamic_index_in_dim(value, c, 0, keepdims=False)[0]
        give = lax.dynamic_index_in_dim(value, 1 - c, 0, keepdims=False)[0]
        return jnp.concatenate([keep, swap(give, "c", C, 1)], axis=0)

    def from_core(value):
        keep, give = value[:tokens], value[tokens:]
        came = swap(give, "c", C, 1)
        first = jnp.where(c == 0, keep, came)
        second = jnp.where(c == 0, came, keep)
        return jnp.stack([first, second])[:, None]

    inputs = to_core(layer_in)
    rounded_in = inputs.astype(low)
    x_slots = gather_slots(rounded_in, "z", Z)

    packed = jnp.concatenate(
        [
            v.astype(low)
            for v in (
                query_bias,
                value_bias,
                output_bias,
                first_gain,
                first_shift,
                down_bias,
                second_gain,
                second_shift,
                up_bias,
            )
        ]
    )[None]
    vectors = sum_all(
        lax.dynamic_update_slice_in_dim(
            jnp.zeros((devices, packed.shape[1]), low), packed, mine, 0
        ),
        sizes,
    ).astype(wide)
    vector = lambda i: vectors[:, i * rows : (i + 1) * rows].reshape(D)
    by_head = lambda v: lax.dynamic_index_in_dim(v.reshape(heads, Z, DH), z, 1, keepdims=False)
    query_offset, value_offset = by_head(vector(0)), by_head(vector(1))
    (
        output_offset,
        first_scale,
        first_offset,
        down_offset,
        second_scale,
        second_offset,
    ) = (vector(i) for i in range(2, 8))
    up_offset = lax.dynamic_index_in_dim(
        vectors[:, 8 * rows :].reshape(S, slice_width), s, 0, keepdims=False
    )
    qkv_offset = jnp.concatenate(
        [query_offset.reshape(-1), jnp.zeros((heads * DH,), wide), value_offset.reshape(-1)]
    )

    width = 3 * heads * DH
    qkv_local = jnp.stack(
        [query_weight.astype(low), key_weight.astype(low), value_weight.astype(low)], axis=1
    )
    qkv_local = qkv_local.reshape(rows, 3, heads, Z, DH).transpose(3, 0, 1, 2, 4)
    qkv_local = exchange(qkv_local.reshape(Z, rows, width), "z", Z)
    qkv_matrix = lax.all_gather(qkv_local, ("seq", "c"), axis=0, tiled=False)
    qkv_matrix = qkv_matrix.reshape(S, C, Z, rows, width).transpose(0, 2, 1, 3, 4).reshape(D, width)
    if whole_heads:
        output_matrix = lax.all_gather(
            output_weight.astype(low), ("seq", "c"), axis=0, tiled=True
        )
    else:
        output_matrix = lax.all_gather(output_weight.astype(low), ALL, axis=0, tiled=True)
        output_matrix = lax.dynamic_index_in_dim(
            output_matrix.reshape(heads, Z, DH, D), z, 1, keepdims=False
        ).reshape(heads * DH, D)
    up_local = up_weight.astype(low).reshape(rows, S, slice_width).transpose(1, 0, 2)
    up_local = exchange(up_local, "seq", S)
    up_matrix = lax.all_gather(up_local, ("z", "c"), axis=0, tiled=False)
    up_matrix = up_matrix.transpose(1, 0, 2, 3).reshape(D, slice_width)
    down_matrix = lax.all_gather(down_weight.astype(low), ("z", "c"), axis=0, tiled=True)

    ids = lax.dynamic_index_in_dim(doc_ids, c, 0, keepdims=False)[0].reshape(Z, C, tokens)
    ids = jnp.where(c == 0, ids, ids[:, ::-1])
    ids = ids[slot_order("z", Z)].reshape(-1)
    row_ids, col_ids = ids[:, None], ids[None, :]

    x_all = jnp.concatenate(x_slots, axis=0)
    qkv = (matmul(x_all, qkv_matrix) + qkv_offset).astype(low)
    mixed, totals = attend(qkv, row_ids, col_ids, heads)
    branch_parts = split_slots(matmul(mixed, output_matrix).astype(low), Z)
    branch = scatter_slots(branch_parts, "z", Z) + output_offset
    hidden, first_normed, first_inverse = normalize_forward(
        inputs + branch, first_scale, first_offset
    )
    hidden_low = hidden.astype(low)

    h_slots = gather_slots(hidden_low, "seq", S)
    actives, slopes, downs = [], [], []
    for h_slot in h_slots:
        active, slope = gelu_both(matmul(h_slot, up_matrix) + up_offset)
        active = active.astype(low)
        actives.append(active)
        slopes.append(slope)
        downs.append(matmul(active, down_matrix).astype(low))
    down = scatter_slots(downs, "seq", S) + down_offset
    result, second_normed, second_inverse = normalize_forward(
        hidden + down, second_scale, second_offset
    )
    layer_out = from_core(result)

    grad_output = to_core(out_grad)
    grad_second, second_gain_part, second_shift_part = normalize_backward(
        grad_output, second_normed, second_inverse, second_scale
    )
    grad_down = grad_second.astype(low)
    g_slots = gather_slots(grad_down, "seq", S)
    grad_ups, hidden_parts = [], []
    for g_slot, slope in zip(g_slots, slopes, strict=True):
        grad_up = (against(g_slot, down_matrix) * slope).astype(low)
        grad_ups.append(grad_up)
        hidden_parts.append(against(grad_up, up_matrix).astype(low))
    grad_hidden = grad_second + scatter_slots(hidden_parts, "seq", S)

    joined = lambda values: jnp.concatenate(values, axis=0)
    down_term = transposed(joined(actives), joined(g_slots)).astype(low)
    down_weight_grad = lax.psum_scatter(
        down_term, ("z", "c"), scatter_dimension=0, tiled=True
    ).astype(wide)
    grad_up_all = joined(grad_ups)
    up_term = transposed(joined(h_slots), grad_up_all).astype(low)
    up_term = up_term.reshape(S, F, rows, slice_width).transpose(1, 0, 2, 3)
    up_mine = lax.psum_scatter(
        up_term.reshape(D, slice_width), ("z", "c"), scatter_dimension=0, tiled=True
    )
    up_mine = exchange(up_mine.reshape(S, rows, slice_width), "seq", S)
    up_weight_grad = up_mine.transpose(1, 0, 2).reshape(rows, hidden_units).astype(wide)

    grad_first, first_gain_part, first_shift_part = normalize_backward(
        grad_hidden, first_normed, first_inverse, first_scale
    )
    grad_branch = grad_first.astype(low)
    b_all = joined(gather_slots(grad_branch, "z", Z))
    grad_mixed = against(b_all, output_matrix).astype(low)
    grad_query, grad_key, grad_value = attend_back(
        qkv, grad_mixed, totals, row_ids, col_ids, heads
    )
    grad_qkv = jnp.concatenate([grad_query, grad_key, grad_value], axis=1)
    in_parts = split_slots(against(grad_qkv, qkv_matrix).astype(low), Z)
    input_grad = from_core(grad_first + scatter_slots(in_parts, "z", Z))

    qkv_term = transposed(x_all, grad_qkv).astype(low)
    qkv_term = qkv_term.reshape(S, Z, C, rows, width).transpose(0, 2, 1, 3, 4)
    qkv_mine = lax.psum_scatter(
        qkv_term.reshape(D, width), ("seq", "c"), scatter_dimension=0, tiled=True
    )
    qkv_mine = exchange(qkv_mine.reshape(Z, rows, width), "z", Z).reshape(Z, rows, 3, heads, DH)
    qkv_grads = qkv_mine.transpose(2, 1, 3, 0, 4).reshape(3, rows, D).astype(wide)
    output_term = transposed(mixed, b_all).astype(low)
    if whole_heads:
        output_weight_grad = lax.psum_scatter(
            output_term, ("seq", "c"), scatter_dimension=0, tiled=True
        ).astype(wide)
    else:
        output_term = lax.dynamic_update_slice_in_dim(
            jnp.zeros((heads, Z, DH, D), low), output_term.reshape(heads, 1, DH, D), z, 1
        )
        output_weight_grad = lax.psum_scatter(
            output_term.reshape(D, D), ALL, scatter_dimension=0, tiled=True
        ).astype(wide)

    spread = lambda v: lax.dynamic_update_slice_in_dim(
        jnp.zeros((heads, Z, DH), wide), v.reshape(heads, 1, DH), z, 1
    ).reshape(devices, rows)
    up_part = lax.dynamic_update_slice_in_dim(
        jnp.zeros((S, slice_width), wide), column_sum(grad_up_all)[None], s, 0
    ).reshape(devices, share)
    terms = [
        spread(column_sum(grad_query)),
        spread(column_sum(grad_value)),
        column_sum(grad_branch).reshape(devices, rows),
        first_gain_part.reshape(devices, rows),
        first_shift_part.reshape(devices, rows),
        column_sum(grad_down).reshape(devices, rows),
        second_gain_part.reshape(devices, rows),
        second_shift_part.reshape(devices, rows),
        up_part,
    ]
    sums = lax.dynamic_index_in_dim(
        sum_all(jnp.concatenate(terms, axis=1), sizes), mine, 0, keepdims=False
    )
    vec = lambda i: sums[i * rows : (i + 1) * rows]
    return (
        layer_out,
        input_grad,
        qkv_grads[0],
        vec(0),
        qkv_grads[1],
        qkv_grads[2],
        vec(1),
        output_weight_grad,
        vec(2),
        vec(3),
        vec(4),
        up_weight_grad,
        sums[8 * rows :],
        down_weight_grad,
        vec(5),
        vec(6),
        vec(7),
    )


def solution(mesh):
    sizes = {"seq": mesh.shape["seq"], "z": mesh.shape["fsdp"] // CORES, "c": CORES}
    inner = Mesh(mesh.devices.reshape(tuple(sizes[a] for a in ALL)), ALL)
    token = P(None, "seq", ("z", "c"), None)
    matrix = P(ALL, None)
    vector = P(ALL)
    return jax.shard_map(
        functools.partial(shards, sizes),
        mesh=inner,
        in_specs=(
            token,
            P(None, "seq", None),
            token,
            matrix,
            vector,
            matrix,
            matrix,
            vector,
            matrix,
            vector,
            vector,
            vector,
            matrix,
            vector,
            matrix,
            vector,
            vector,
            vector,
        ),
        out_specs=(
            token,
            token,
            matrix,
            vector,
            matrix,
            matrix,
            vector,
            matrix,
            vector,
            vector,
            vector,
            matrix,
            vector,
            matrix,
            vector,
            vector,
            vector,
        ),
        check_vma=False,
    )
```

```python
import functools

import jax
import jax.numpy as jnp
from jax import lax
from jax.experimental import pallas as pl
from jax.experimental.pallas import tpu as pltpu
from jax.sharding import Mesh
from jax.sharding import PartitionSpec as P

D = 2048
H = 16
DH = 128
MB = 2
CORES = 2

low = jnp.bfloat16
wide = jnp.float32
norm_eps = 1e-06
masked_score = -1e30
score_scale = DH ** (-0.5)
ALL = ("seq", "z", "c")


def normalize_forward(summed, gain_vector, shift_vector):
    center = summed - jnp.mean(summed, axis=-1, keepdims=True)
    inverse = lax.rsqrt(jnp.mean(center * center, axis=-1, keepdims=True) + norm_eps)
    normed = center * inverse
    return (normed * gain_vector + shift_vector, normed, inverse)


def normalize_backward(grad_output, normed, inverse, gain_vector):
    grad_normed = grad_output * gain_vector
    centered = grad_normed - jnp.mean(grad_normed, axis=-1, keepdims=True)
    grad_input = inverse * (
        centered - normed * jnp.mean(grad_normed * normed, axis=-1, keepdims=True)
    )
    return (grad_input, jnp.sum(grad_output * normed, axis=0), jnp.sum(grad_output, axis=0))


def matmul(left, right):
    return jnp.dot(left, right, preferred_element_type=wide)


def transposed(left, right):
    return jnp.einsum("ti,tj->ij", left, right, preferred_element_type=wide)


def against(left, right):
    return jnp.einsum("ti,ji->tj", left, right, preferred_element_type=wide)


def column_sum(matrix):
    return jnp.sum(matrix.astype(wide), axis=0)


def gelu_both(u):
    root = (2.0 / jnp.pi) ** 0.5
    cubic = 0.044715
    square = u * u
    bend = jnp.tanh(root * (u + cubic * u * square))
    half = 0.5 * (1.0 + bend)
    slope = half + 0.5 * u * (1.0 - bend * bend) * (root * (1.0 + 3.0 * cubic * square))
    return u * half, slope


def nt(left, right):
    return lax.dot_general(left, right, (((1,), (1,)), ((), ())), preferred_element_type=wide)


def tn(left, right):
    return lax.dot_general(left, right, (((0,), (0,)), ((), ())), preferred_element_type=wide)


def attend_kernel(rows, q_ref, k_ref, v_ref, row_ref, col_ref, o_ref, total_ref):
    keys = k_ref[...]
    values = v_ref[...]
    cols = col_ref[...]
    for start in range(0, q_ref.shape[0], rows):
        here = pl.ds(start, rows)
        scores = nt(q_ref[here, :], keys) * score_scale
        scores = jnp.where(row_ref[here, :] == cols, scores, masked_score)
        top = jnp.max(scores, axis=-1, keepdims=True)
        raised = jnp.exp(scores - top)
        total = jnp.sum(raised, axis=-1, keepdims=True)
        probs = (raised * (1.0 / total)).astype(low)
        o_ref[here, :] = jnp.dot(probs, values, preferred_element_type=wide).astype(low)
        total_ref[0, here, :] = top + jnp.log(total)


def attend_back_kernel(
    rows, q_ref, k_ref, v_ref, g_ref, total_ref, row_ref, col_ref, dq_ref, dk_ref, dv_ref, ka, va
):
    keys = k_ref[...]
    values = v_ref[...]
    cols = col_ref[...]
    for start in range(0, q_ref.shape[0], rows):
        here = pl.ds(start, rows)
        queries = q_ref[here, :]
        grads = g_ref[here, :]
        scores = nt(queries, keys) * score_scale
        scores = jnp.where(row_ref[here, :] == cols, scores, masked_score)
        probs = jnp.exp(scores - total_ref[0, here, :])
        grad_probs = nt(grads, values)
        row_dot = jnp.sum(probs * grad_probs, axis=-1, keepdims=True)
        grad_scores = (probs * (grad_probs - row_dot)).astype(low)
        dq_ref[here, :] = (
            jnp.dot(grad_scores, keys, preferred_element_type=wide) * score_scale
        ).astype(low)
        dk_part = tn(grad_scores, queries)
        dv_part = tn(probs.astype(low), grads)
        if start == 0:
            ka[...] = dk_part
            va[...] = dv_part
        else:
            ka[...] += dk_part
            va[...] += dv_part
    dk_ref[...] = (ka[...] * score_scale).astype(low)
    dv_ref[...] = va[...].astype(low)


def attend(qkv, row_ids, col_ids, heads):
    length = qkv.shape[0]
    rows = min(256, length)
    block = lambda part: pl.BlockSpec((length, DH), lambda h: (0, part * heads + h))
    return pl.pallas_call(
        functools.partial(attend_kernel, rows),
        grid=(heads,),
        in_specs=[
            block(0),
            block(1),
            block(2),
            pl.BlockSpec((length, 1), lambda h: (0, 0)),
            pl.BlockSpec((1, length), lambda h: (0, 0)),
        ],
        out_specs=[
            pl.BlockSpec((length, DH), lambda h: (0, h)),
            pl.BlockSpec((1, length, 1), lambda h: (h, 0, 0)),
        ],
        out_shape=[
            jax.ShapeDtypeStruct((length, heads * DH), low),
            jax.ShapeDtypeStruct((heads, length, 1), wide),
        ],
        cost_estimate=pl.CostEstimate(
            flops=4 * heads * length * length * DH,
            bytes_accessed=8 * heads * length * DH,
            transcendentals=heads * length * length,
        ),
        compiler_params=pltpu.CompilerParams(vmem_limit_bytes=40 * 2**20),
        name="attend",
    )(qkv, qkv, qkv, row_ids, col_ids)


def attend_back(qkv, grad_mixed, totals, row_ids, col_ids, heads):
    length = qkv.shape[0]
    rows = min(256, length)
    block = lambda part: pl.BlockSpec((length, DH), lambda h: (0, part * heads + h))
    out = pl.BlockSpec((length, DH), lambda h: (0, h))
    shape = jax.ShapeDtypeStruct((length, heads * DH), low)
    return pl.pallas_call(
        functools.partial(attend_back_kernel, rows),
        grid=(heads,),
        in_specs=[
            block(0),
            block(1),
            block(2),
            out,
            pl.BlockSpec((1, length, 1), lambda h: (h, 0, 0)),
            pl.BlockSpec((length, 1), lambda h: (0, 0)),
            pl.BlockSpec((1, length), lambda h: (0, 0)),
        ],
        out_specs=[out, out, out],
        out_shape=[shape, shape, shape],
        scratch_shapes=[pltpu.VMEM((length, DH), wide), pltpu.VMEM((length, DH), wide)],
        cost_estimate=pl.CostEstimate(
            flops=10 * heads * length * length * DH,
            bytes_accessed=16 * heads * length * DH,
            transcendentals=heads * length * length,
        ),
        compiler_params=pltpu.CompilerParams(vmem_limit_bytes=48 * 2**20),
        name="attend_back",
    )(qkv, qkv, qkv, grad_mixed, totals, row_ids, col_ids)


def swap(value, axis, size, bit):
    return lax.ppermute(value, axis, [(i, i ^ bit) for i in range(size)])


def together(*values):
    return lax.optimization_barrier(values)


def trade(value, axis, size):
    here = lax.axis_index(axis)
    pick = lambda i: lax.dynamic_index_in_dim(value, i, 0, keepdims=False)
    return [pick(here)] + [swap(pick(here ^ k), axis, size, k) for k in range(1, size)]


def ordered(came, axis):
    here = lax.axis_index(axis)
    size = len(came)
    return jnp.stack([lax.select_n(here, *(came[i ^ k] for k in range(size))) for i in range(size)])


def exchange(value, axis, size):
    return ordered(trade(value, axis, size), axis)


def bits(size):
    step = 1
    while step < size:
        yield step
        step *= 2


def sum_over(value, axes, sizes):
    for axis in axes:
        for bit in bits(sizes[axis]):
            value = value + swap(value, axis, sizes[axis], bit)
    return value


ENDS = [(0, 1), (1, 0), (2, 3), (3, 2)]
MIDDLE = [(1, 2), (2, 1)]
OUTWARD = [(1, 0), (2, 3)]
INWARD = [(0, 1), (3, 2)]


def send(value, pairs):
    return lax.ppermute(value, "z", pairs)


def add(left, right):
    return (left.astype(wide) + right.astype(wide)).astype(low)


def spread_1(own):
    return own, send(own, ENDS), send(own, MIDDLE)


def spread_2(own, first, third):
    return own, first, send(first, MIDDLE), send(third, OUTWARD), third


def spread_3(own, first, second_in, second_out, third_in):
    inner = (lax.axis_index("z") == 1) | (lax.axis_index("z") == 2)
    third_out = send(second_in, OUTWARD)
    return [
        own,
        first,
        jnp.where(inner, second_in, second_out),
        jnp.where(inner, third_in, third_out),
    ]


def sum_1(own, first, second, third):
    second_came = send(second, INWARD)
    first_came = send(add(second, send(third, INWARD)), MIDDLE)
    second_came, first_came = together(second_came, first_came)
    return own, add(first, first_came), add(third, second_came)


def sum_2(own, first, third):
    from_end, from_middle = send(first, ENDS), send(third, MIDDLE)
    return own.astype(wide) + from_middle.astype(wide) + from_end.astype(wide)


def gather_slots(own, axis, size):
    if size != 4:
        whole = lax.all_gather(own, axis, axis=0)
        return [whole[i] for i in range(size)]
    if axis == "z":
        return spread_3(*spread_2(*spread_1(own)))
    half = own.shape[0] // 2
    first = swap(own, axis, 4, 1)
    second = swap(own, axis, 4, 2)
    third_top = swap(first[:half], axis, 4, 2)
    third_end = swap(second[half:], axis, 4, 1)
    return [own, first, second, jnp.concatenate([third_top, third_end], axis=0)]


def scatter_slots(parts, axis, size):
    if size != 4:
        return lax.psum_scatter(jnp.stack(parts), axis, scatter_dimension=0, tiled=False).astype(
            wide
        )
    if axis == "z":
        return sum_2(*sum_1(*parts))
    own, first, second, third = parts
    half = own.shape[0] // 2
    top = swap(third[:half], axis, 4, 2)
    end = swap(third[half:], axis, 4, 1)
    first_full = jnp.concatenate([add(first[:half], top), first[half:]], axis=0)
    second_full = jnp.concatenate([second[:half], add(second[half:], end)], axis=0)
    from_first = swap(first_full, axis, 4, 1)
    from_second = swap(second_full, axis, 4, 2)
    return own.astype(wide) + from_first.astype(wide) + from_second.astype(wide)


def slot_order(axis, size):
    order = jnp.arange(size)
    return order ^ lax.axis_index(axis) if size == 4 else order


def split_slots(value, size):
    step = value.shape[0] // size
    return [value[i * step : (i + 1) * step] for i in range(size)]


def shards(
    sizes,
    layer_in,
    doc_ids,
    out_grad,
    query_weight,
    query_bias,
    key_weight,
    value_weight,
    value_bias,
    output_weight,
    output_bias,
    first_gain,
    first_shift,
    up_weight,
    up_bias,
    down_weight,
    down_bias,
    second_gain,
    second_shift,
):
    S, Z, C = sizes["seq"], sizes["z"], sizes["c"]
    devices = S * Z * C
    s, z, c = (lax.axis_index(a) for a in ALL)
    rows = query_weight.shape[0]
    hidden_units = up_weight.shape[1]
    share = hidden_units // devices
    slice_width = hidden_units // Z
    heads = H // Z
    tokens = layer_in.shape[2]
    whole_heads = rows * C == DH and H == S * Z
    cross = lambda value: swap(value, "c", C, 1)
    pick = lambda value, axis, i: lax.dynamic_index_in_dim(value, i, axis, keepdims=False)

    def place(value, axis, size, i):
        shape = list(value.shape)
        shape.insert(axis, size)
        start = [0] * len(shape)
        start[axis] = i
        return lax.dynamic_update_slice(
            jnp.zeros(shape, value.dtype), jnp.expand_dims(value, axis), start
        )

    def to_core(value):
        return jnp.concatenate([pick(value, 0, c)[0], cross(pick(value, 0, 1 - c)[0])], axis=0)

    def from_core(value):
        keep, came = value[:tokens], cross(value[tokens:])
        first = jnp.where(c == 0, keep, came)
        second = jnp.where(c == 0, came, keep)
        return jnp.stack([first, second])[:, None]

    def gather_rows(local):
        whole = lax.all_gather(
            local.reshape(-1, local.shape[2]), ("seq", "c"), axis=0, tiled=False
        )
        return whole.reshape(S, C, *local.shape).transpose(0, 2, 1, 3, 4)

    def by_owner(term):
        return term.reshape(S, Z, C, rows, -1).transpose(0, 2, 1, 3, 4).reshape(D, -1)

    width = 3 * heads * DH
    qkv_local = jnp.stack(
        [query_weight.astype(low), key_weight.astype(low), value_weight.astype(low)], axis=1
    )
    qkv_local = qkv_local.reshape(rows, 3, heads, Z, DH).transpose(3, 0, 1, 2, 4)
    own_vectors = [query_bias, value_bias, output_bias, first_gain, first_shift]
    own_vectors += [down_bias, second_gain, second_shift, up_bias]
    own_vectors = jnp.concatenate([v.astype(low) for v in own_vectors])
    extra = jnp.pad(own_vectors[None], ((0, 7), (0, width - own_vectors.shape[0])))
    qkv_local = jnp.concatenate(
        [qkv_local.reshape(Z, rows, width), jnp.broadcast_to(extra, (Z, 8, width))], axis=1
    )
    rounded_in, qkv_local = together(to_core(layer_in.astype(low)), qkv_local)
    gathered = gather_rows(exchange(qkv_local, "z", Z))
    if Z == 4:
        x_blocks, gathered = together(spread_2(*spread_1(rounded_in)), gathered)
        x_slots = spread_3(*x_blocks)
    else:
        x_slots = gather_slots(rounded_in, "z", Z)
    qkv_matrix = gathered[:, :, :, :rows].reshape(D, width)
    vectors = gathered[:, :, :, rows].reshape(devices, width)[:, : own_vectors.shape[0]]
    vectors = vectors.astype(wide)

    if whole_heads:
        output_matrix = lax.all_gather(
            output_weight.astype(low), ("seq", "c"), axis=0, tiled=True
        )
    else:
        output_matrix = lax.all_gather(output_weight.astype(low), ALL, axis=0, tiled=True)
        output_matrix = pick(output_matrix.reshape(heads, Z, DH, D), 1, z).reshape(heads * DH, D)
    down_matrix = lax.all_gather(down_weight.astype(low), ("seq", "c"), axis=0, tiled=True)

    up_local = up_weight.astype(low).reshape(rows, S, Z, C * share).transpose(2, 0, 1, 3)
    up_local = up_local.reshape(Z, rows, slice_width)
    x_slots, up_local, layer_in, out_grad, qkv_matrix, vectors = together(
        x_slots, up_local, layer_in, out_grad, qkv_matrix, vectors
    )
    inputs, grad_output = to_core(layer_in), to_core(out_grad)
    up_came = trade(up_local, "z", Z)

    vector = lambda i: vectors[:, i * rows : (i + 1) * rows].reshape(D)
    query_offset, value_offset = (
        pick(vector(i).reshape(heads, Z, DH), 1, z).reshape(heads * DH) for i in range(2)
    )
    (
        output_offset,
        first_scale,
        first_offset,
        down_offset,
        second_scale,
        second_offset,
    ) = (vector(i) for i in range(2, 8))
    up_offset = vectors[:, 8 * rows :].reshape(S, Z, C, share)
    up_offset = pick(up_offset, 1, z).reshape(slice_width)
    qkv_offset = jnp.concatenate([query_offset, jnp.zeros((heads * DH,), wide), value_offset])

    ids = pick(doc_ids, 0, c)[0].reshape(Z, C, tokens)
    ids = jnp.where(c == 0, ids, ids[:, ::-1])
    ids = ids[slot_order("z", Z)].reshape(-1)
    row_ids, col_ids = ids[:, None], ids[None, :]

    x_all = jnp.concatenate(x_slots, axis=0)
    qkv = (matmul(x_all, qkv_matrix) + qkv_offset).astype(low)
    mixed, totals = attend(qkv, row_ids, col_ids, heads)
    up_came, mixed = together(up_came, mixed)
    up_matrix = gather_rows(ordered(up_came, "z")).reshape(D, slice_width)
    branch_parts = split_slots(matmul(mixed, output_matrix).astype(low), Z)
    branch = scatter_slots(branch_parts, "z", Z) + output_offset
    hidden, first_normed, first_inverse = normalize_forward(
        inputs + branch, first_scale, first_offset
    )
    hidden_low = hidden.astype(low)

    def forward(h_slot):
        active, slope = gelu_both(matmul(h_slot, up_matrix) + up_offset)
        active = active.astype(low)
        return active, slope, lax.optimization_barrier(matmul(active, down_matrix).astype(low))

    if Z == 4:
        h_blocks, up_matrix, down_matrix = together(
            spread_1(hidden_low), up_matrix, down_matrix
        )
        h_blocks, done_0 = together(spread_2(*h_blocks), forward(hidden_low))
        h_slots, done_1 = together(spread_3(*h_blocks), forward(h_blocks[1]))
        done = [done_0, done_1, forward(h_slots[2]), forward(h_slots[3])]
    else:
        h_slots = gather_slots(hidden_low, "z", Z)
        done = [forward(h_slot) for h_slot in h_slots]
    actives, slopes, downs = zip(*done, strict=True)
    down = scatter_slots(downs, "z", Z) + down_offset
    result, second_normed, second_inverse = normalize_forward(
        hidden + down, second_scale, second_offset
    )

    grad_second, second_gain_part, second_shift_part = normalize_backward(
        grad_output, second_normed, second_inverse, second_scale
    )
    grad_down = grad_second.astype(low)
    g_slots = gather_slots(grad_down, "z", Z)
    grad_ups, hidden_parts = [], []
    for g_slot, slope in zip(g_slots, slopes, strict=True):
        grad_up = (against(g_slot, down_matrix) * slope).astype(low)
        grad_ups.append(grad_up)
        hidden_parts.append(lax.optimization_barrier(against(grad_up, up_matrix).astype(low)))

    joined = lambda values: jnp.concatenate(values, axis=0)
    grad_up_all = joined(grad_ups)
    down_term = transposed(joined(actives), joined(g_slots)).astype(low)
    up_term = transposed(joined(h_slots), grad_up_all).astype(low)
    if Z == 4:
        hidden_parts, down_term = together(sum_1(*hidden_parts), down_term)
        hidden_sum = sum_2(*hidden_parts)
    else:
        hidden_sum = scatter_slots(hidden_parts, "z", Z)
    down_mine = lax.psum_scatter(down_term, ("seq", "c"), scatter_dimension=0, tiled=True)
    grad_hidden = grad_second + hidden_sum

    grad_first, first_gain_part, first_shift_part = normalize_backward(
        grad_hidden, first_normed, first_inverse, first_scale
    )
    grad_branch = grad_first.astype(low)
    terms = [
        column_sum(grad_branch),
        first_gain_part,
        first_shift_part,
        column_sum(grad_down),
        second_gain_part,
        second_shift_part,
    ]
    terms = jnp.concatenate([v.reshape(devices, rows) for v in terms], axis=1).astype(low)
    below = -(-terms.size // D // 8) * 8
    terms = jnp.pad(terms.reshape(-1), (0, below * D - terms.size)).reshape(below, D)
    sent = jnp.concatenate([grad_branch, terms], axis=0)
    if Z == 4:
        b_blocks, up_term = together(spread_1(sent), by_owner(up_term))
        b_slots = spread_3(*spread_2(*b_blocks))
    else:
        b_slots, up_term = gather_slots(sent, "z", Z), by_owner(up_term)
    up_mine = lax.psum_scatter(up_term, ("seq", "c"), scatter_dimension=0, tiled=True)
    b_all = joined([v[:-below] for v in b_slots])
    term_sums = sum(v[-below:].astype(wide) for v in b_slots)
    term_sums = term_sums.reshape(-1)[: 6 * D].reshape(S, Z, C, 6 * rows)
    term_sums = pick(term_sums, 1, z)
    grad_mixed = against(b_all, output_matrix).astype(low)
    grad_query, grad_key, grad_value = attend_back(
        qkv, grad_mixed, totals, row_ids, col_ids, heads
    )
    grad_qkv = jnp.concatenate([grad_query, grad_key, grad_value], axis=1)
    in_parts = split_slots(against(grad_qkv, qkv_matrix).astype(low), Z)
    in_parts, grad_qkv_late, mixed_late, down_mine, term_sums = together(
        in_parts, grad_qkv, mixed, down_mine, term_sums
    )
    if Z == 4:
        in_parts, up_mine = together(sum_1(*in_parts), up_mine)
        in_sum = sum_2(*in_parts)
    else:
        in_sum = scatter_slots(in_parts, "z", Z)
    layer_out = from_core(result)
    input_grad = from_core(grad_first + in_sum)
    down_weight_grad = down_mine.astype(wide)
    up_mine = exchange(up_mine.reshape(Z, rows, slice_width), "z", Z)
    up_mine = up_mine.reshape(Z, rows, S, C * share)
    up_weight_grad = up_mine.transpose(1, 2, 0, 3).reshape(rows, hidden_units).astype(wide)

    def in_plane(term, rest):
        term = term.reshape(S, -1, C, rows, rest)
        both = add(pick(term, 2, c), cross(pick(term, 2, 1 - c))).reshape(S, -1, rest)
        parts = [both[i] for i in range(S)] if S != 4 else [pick(both, 0, s ^ k) for k in range(S)]
        return scatter_slots(parts, "seq", S)

    output_term = transposed(mixed_late, b_all).astype(low)
    if whole_heads:
        output_weight_grad = in_plane(output_term, D)
    else:
        output_term = place(output_term.reshape(heads, DH, D), 1, Z, z)
        output_weight_grad = lax.psum_scatter(
            output_term.reshape(D, D), ALL, scatter_dimension=0, tiled=True
        ).astype(wide)
    qkv_mine = in_plane(transposed(x_all, grad_qkv_late).astype(low), width).astype(low)
    qkv_mine = exchange(qkv_mine.reshape(Z, rows, width), "z", Z)
    qkv_grads = qkv_mine.reshape(Z, rows, 3, heads, DH).transpose(2, 1, 3, 0, 4)
    qkv_grads = qkv_grads.reshape(3, rows, D).astype(wide)

    sums = sum_over(term_sums, ("c", "seq"), sizes)
    sums = pick(pick(sums, 0, s), 0, c)
    vec = lambda i: sums[i * rows : (i + 1) * rows]
    up_bias_grad = sum_over(column_sum(grad_up_all).reshape(S, C, share), ("c", "seq"), sizes)
    up_bias_grad = pick(pick(up_bias_grad, 0, s), 0, c)
    biases = column_sum(grad_qkv_late).reshape(3, heads * DH)
    biases = jnp.stack([biases[0], biases[2]])
    biases = sum_over(biases, ("c", "seq"), sizes)
    if whole_heads:
        biases = pick(pick(biases.reshape(2, S, C, rows), 1, s), 1, c)
    else:
        biases = lax.all_gather(biases.reshape(2, heads, DH), "z", axis=2, tiled=False)
        biases = pick(biases.reshape(2, devices, rows), 1, (s * Z + z) * C + c)
    return (
        layer_out,
        input_grad,
        qkv_grads[0],
        biases[0],
        qkv_grads[1],
        qkv_grads[2],
        biases[1],
        output_weight_grad,
        vec(0),
        vec(1),
        vec(2),
        up_weight_grad,
        up_bias_grad,
        down_weight_grad,
        vec(3),
        vec(4),
        vec(5),
    )


def solution(mesh):
    sizes = {"seq": mesh.shape["seq"], "z": mesh.shape["fsdp"] // CORES, "c": CORES}
    inner = Mesh(mesh.devices.reshape(tuple(sizes[a] for a in ALL)), ALL)
    token = P(None, "seq", ("z", "c"), None)
    matrix = P(ALL, None)
    vector = P(ALL)
    return jax.shard_map(
        functools.partial(shards, sizes),
        mesh=inner,
        in_specs=(
            token,
            P(None, "seq", None),
            token,
            matrix,
            vector,
            matrix,
            matrix,
            vector,
            matrix,
            vector,
            vector,
            vector,
            matrix,
            vector,
            matrix,
            vector,
            vector,
            vector,
        ),
        out_specs=(
            token,
            token,
            matrix,
            vector,
            matrix,
            matrix,
            vector,
            matrix,
            vector,
            vector,
            vector,
            matrix,
            vector,
            matrix,
            vector,
            vector,
            vector,
        ),
        check_vma=False,
    )
```

```python
import functools

import jax
import jax.numpy as jnp
from jax import lax
from jax.experimental import pallas as pl
from jax.experimental.pallas import tpu as pltpu
from jax.sharding import Mesh
from jax.sharding import PartitionSpec as P

D = 2048
H = 16
DH = 128
MB = 2
CORES = 2

low = jnp.bfloat16
wide = jnp.float32
norm_eps = 1e-06
masked_score = -1e30
score_scale = DH ** (-0.5)
ALL = ("seq", "z", "c")


def normalize_forward(summed, gain_vector, shift_vector):
    center = summed - jnp.mean(summed, axis=-1, keepdims=True)
    inverse = lax.rsqrt(jnp.mean(center * center, axis=-1, keepdims=True) + norm_eps)
    normed = center * inverse
    return (normed * gain_vector + shift_vector, normed, inverse)


def normalize_backward(grad_output, normed, inverse, gain_vector):
    grad_normed = grad_output * gain_vector
    centered = grad_normed - jnp.mean(grad_normed, axis=-1, keepdims=True)
    grad_input = inverse * (
        centered - normed * jnp.mean(grad_normed * normed, axis=-1, keepdims=True)
    )
    return (grad_input, jnp.sum(grad_output * normed, axis=0), jnp.sum(grad_output, axis=0))


def matmul(left, right):
    return jnp.dot(left, right, preferred_element_type=wide)


def transposed(left, right):
    return jnp.einsum("ti,tj->ij", left, right, preferred_element_type=wide)


def against(left, right):
    return jnp.einsum("ti,ji->tj", left, right, preferred_element_type=wide)


def column_sum(matrix):
    return jnp.sum(matrix.astype(wide), axis=0)


def gelu_both(u):
    root = (2.0 / jnp.pi) ** 0.5
    cubic = 0.044715
    square = u * u
    bend = jnp.tanh(root * (u + cubic * u * square))
    half = 0.5 * (1.0 + bend)
    slope = half + 0.5 * u * (1.0 - bend * bend) * (root * (1.0 + 3.0 * cubic * square))
    return u * half, slope


def nt(left, right):
    return lax.dot_general(left, right, (((1,), (1,)), ((), ())), preferred_element_type=wide)


def tn(left, right):
    return lax.dot_general(left, right, (((0,), (0,)), ((), ())), preferred_element_type=wide)


def attend_kernel(rows, q_ref, k_ref, v_ref, row_ref, col_ref, o_ref, total_ref):
    keys = k_ref[...]
    values = v_ref[...]
    cols = col_ref[...]
    for start in range(0, q_ref.shape[0], rows):
        here = pl.ds(start, rows)
        scores = nt(q_ref[here, :], keys) * score_scale
        scores = jnp.where(row_ref[here, :] == cols, scores, masked_score)
        top = jnp.max(scores, axis=-1, keepdims=True)
        raised = jnp.exp(scores - top)
        total = jnp.sum(raised, axis=-1, keepdims=True)
        probs = (raised * (1.0 / total)).astype(low)
        o_ref[here, :] = jnp.dot(probs, values, preferred_element_type=wide).astype(low)
        total_ref[0, here, :] = top + jnp.log(total)


def attend_back_kernel(
    rows, q_ref, k_ref, v_ref, g_ref, total_ref, row_ref, col_ref, dq_ref, dk_ref, dv_ref, ka, va
):
    keys = k_ref[...]
    values = v_ref[...]
    cols = col_ref[...]
    for start in range(0, q_ref.shape[0], rows):
        here = pl.ds(start, rows)
        queries = q_ref[here, :]
        grads = g_ref[here, :]
        scores = nt(queries, keys) * score_scale
        scores = jnp.where(row_ref[here, :] == cols, scores, masked_score)
        probs = jnp.exp(scores - total_ref[0, here, :])
        grad_probs = nt(grads, values)
        row_dot = jnp.sum(probs * grad_probs, axis=-1, keepdims=True)
        grad_scores = (probs * (grad_probs - row_dot)).astype(low)
        dq_ref[here, :] = (
            jnp.dot(grad_scores, keys, preferred_element_type=wide) * score_scale
        ).astype(low)
        dk_part = tn(grad_scores, queries)
        dv_part = tn(probs.astype(low), grads)
        if start == 0:
            ka[...] = dk_part
            va[...] = dv_part
        else:
            ka[...] += dk_part
            va[...] += dv_part
    dk_ref[...] = (ka[...] * score_scale).astype(low)
    dv_ref[...] = va[...].astype(low)


def attend(qkv, row_ids, col_ids, heads):
    length = qkv.shape[0]
    rows = min(256, length)
    block = lambda part: pl.BlockSpec((length, DH), lambda h: (0, part * heads + h))
    return pl.pallas_call(
        functools.partial(attend_kernel, rows),
        grid=(heads,),
        in_specs=[
            block(0),
            block(1),
            block(2),
            pl.BlockSpec((length, 1), lambda h: (0, 0)),
            pl.BlockSpec((1, length), lambda h: (0, 0)),
        ],
        out_specs=[
            pl.BlockSpec((length, DH), lambda h: (0, h)),
            pl.BlockSpec((1, length, 1), lambda h: (h, 0, 0)),
        ],
        out_shape=[
            jax.ShapeDtypeStruct((length, heads * DH), low),
            jax.ShapeDtypeStruct((heads, length, 1), wide),
        ],
        cost_estimate=pl.CostEstimate(
            flops=4 * heads * length * length * DH,
            bytes_accessed=8 * heads * length * DH,
            transcendentals=heads * length * length,
        ),
        compiler_params=pltpu.CompilerParams(vmem_limit_bytes=40 * 2**20),
        name="attend",
    )(qkv, qkv, qkv, row_ids, col_ids)


def attend_back(qkv, grad_mixed, totals, row_ids, col_ids, heads):
    length = qkv.shape[0]
    rows = min(256, length)
    block = lambda part: pl.BlockSpec((length, DH), lambda h: (0, part * heads + h))
    out = pl.BlockSpec((length, DH), lambda h: (0, h))
    shape = jax.ShapeDtypeStruct((length, heads * DH), low)
    return pl.pallas_call(
        functools.partial(attend_back_kernel, rows),
        grid=(heads,),
        in_specs=[
            block(0),
            block(1),
            block(2),
            out,
            pl.BlockSpec((1, length, 1), lambda h: (h, 0, 0)),
            pl.BlockSpec((length, 1), lambda h: (0, 0)),
            pl.BlockSpec((1, length), lambda h: (0, 0)),
        ],
        out_specs=[out, out, out],
        out_shape=[shape, shape, shape],
        scratch_shapes=[pltpu.VMEM((length, DH), wide), pltpu.VMEM((length, DH), wide)],
        cost_estimate=pl.CostEstimate(
            flops=10 * heads * length * length * DH,
            bytes_accessed=16 * heads * length * DH,
            transcendentals=heads * length * length,
        ),
        compiler_params=pltpu.CompilerParams(vmem_limit_bytes=48 * 2**20),
        name="attend_back",
    )(qkv, qkv, qkv, grad_mixed, totals, row_ids, col_ids)


def branch_kernel(*refs):
    *mixed_refs, w_ref, x_ref, own_ref, vector_ref = refs[:-4]
    low_ref, hidden_ref, normed_ref, inverse_ref = refs[-4:]
    branch = vector_ref[0:1, :]
    for k, mixed_ref in enumerate(mixed_refs):
        branch = branch + jnp.dot(mixed_ref[...], w_ref[k], preferred_element_type=wide)
    here = pl.program_id(0) == 0
    tokens = jnp.where(here, own_ref[...], x_ref[...].astype(wide))
    hidden, normed, inverse = normalize_forward(
        tokens + branch, vector_ref[1:2, :], vector_ref[2:3, :]
    )
    low_ref[...] = hidden.astype(low)

    @pl.when(here)
    def _():
        hidden_ref[...] = hidden
        normed_ref[...] = normed
        inverse_ref[...] = inverse


def branch_norm(mixed_slots, weights, x_all, own, vectors):
    size = len(mixed_slots)
    block, width = own.shape
    fed = mixed_slots[0].shape[1]
    row = pl.BlockSpec((block, width), lambda i: (i, 0))
    kept = pl.BlockSpec((block, width), lambda i: (0, 0))
    specs = [pl.BlockSpec((block, fed), lambda i, k=k: (i ^ k, 0)) for k in range(size)]
    return pl.pallas_call(
        branch_kernel,
        grid=(size,),
        in_specs=[
            *specs,
            pl.BlockSpec((size, fed, width), lambda i: (0, 0, 0)),
            row,
            kept,
            pl.BlockSpec(vectors.shape, lambda i: (0, 0)),
        ],
        out_specs=[row, kept, kept, pl.BlockSpec((block, 1), lambda i: (0, 0))],
        out_shape=[
            jax.ShapeDtypeStruct((size * block, width), low),
            jax.ShapeDtypeStruct((block, width), wide),
            jax.ShapeDtypeStruct((block, width), wide),
            jax.ShapeDtypeStruct((block, 1), wide),
        ],
        cost_estimate=pl.CostEstimate(
            flops=2 * size * block * size * fed * width,
            bytes_accessed=2 * size * fed * width + 16 * size * block * width,
            transcendentals=size * block,
        ),
        compiler_params=pltpu.CompilerParams(vmem_limit_bytes=52 * 2**20),
        name="branch_norm",
    )(*mixed_slots, weights, x_all, own, vectors)


def swap(value, axis, size, bit):
    return lax.ppermute(value, axis, [(i, i ^ bit) for i in range(size)])


def together(*values):
    return lax.optimization_barrier(values)


def trade(value, axis, size):
    here = lax.axis_index(axis)
    pick = lambda i: lax.dynamic_index_in_dim(value, i, 0, keepdims=False)
    return [pick(here)] + [swap(pick(here ^ k), axis, size, k) for k in range(1, size)]


def ordered(came, axis):
    here = lax.axis_index(axis)
    size = len(came)
    return jnp.stack([lax.select_n(here, *(came[i ^ k] for k in range(size))) for i in range(size)])


def exchange(value, axis, size):
    return ordered(trade(value, axis, size), axis)


def bits(size):
    step = 1
    while step < size:
        yield step
        step *= 2


def sum_over(value, axes, sizes):
    for axis in axes:
        for bit in bits(sizes[axis]):
            value = value + swap(value, axis, sizes[axis], bit)
    return value


ENDS = [(0, 1), (1, 0), (2, 3), (3, 2)]
MIDDLE = [(1, 2), (2, 1)]
OUTWARD = [(1, 0), (2, 3)]
INWARD = [(0, 1), (3, 2)]


def send(value, pairs):
    return lax.ppermute(value, "z", pairs)


def add(left, right):
    return (left.astype(wide) + right.astype(wide)).astype(low)


def spread_1(own):
    return own, send(own, ENDS), send(own, MIDDLE)


def spread_2(own, first, third):
    return own, first, send(first, MIDDLE), send(third, OUTWARD), third


def spread_3(own, first, second_in, second_out, third_in):
    inner = (lax.axis_index("z") == 1) | (lax.axis_index("z") == 2)
    third_out = send(second_in, OUTWARD)
    return [
        own,
        first,
        jnp.where(inner, second_in, second_out),
        jnp.where(inner, third_in, third_out),
    ]


def sum_1(own, first, second, third):
    second_came = send(second, INWARD)
    first_came = send(add(second, send(third, INWARD)), MIDDLE)
    second_came, first_came = together(second_came, first_came)
    return own, add(first, first_came), add(third, second_came)


def sum_2(own, first, third):
    from_end, from_middle = send(first, ENDS), send(third, MIDDLE)
    return own.astype(wide) + from_middle.astype(wide) + from_end.astype(wide)


def gather_slots(own, axis, size):
    if size != 4:
        whole = lax.all_gather(own, axis, axis=0)
        return [whole[i] for i in range(size)]
    if axis == "z":
        return spread_3(*spread_2(*spread_1(own)))
    half = own.shape[0] // 2
    first = swap(own, axis, 4, 1)
    second = swap(own, axis, 4, 2)
    third_top = swap(first[:half], axis, 4, 2)
    third_end = swap(second[half:], axis, 4, 1)
    return [own, first, second, jnp.concatenate([third_top, third_end], axis=0)]


def scatter_slots(parts, axis, size):
    if size != 4:
        return lax.psum_scatter(jnp.stack(parts), axis, scatter_dimension=0, tiled=False).astype(
            wide
        )
    if axis == "z":
        return sum_2(*sum_1(*parts))
    own, first, second, third = parts
    half = own.shape[0] // 2
    top = swap(third[:half], axis, 4, 2)
    end = swap(third[half:], axis, 4, 1)
    first_full = jnp.concatenate([add(first[:half], top), first[half:]], axis=0)
    second_full = jnp.concatenate([second[:half], add(second[half:], end)], axis=0)
    from_first = swap(first_full, axis, 4, 1)
    from_second = swap(second_full, axis, 4, 2)
    return own.astype(wide) + from_first.astype(wide) + from_second.astype(wide)


def slot_order(axis, size):
    order = jnp.arange(size)
    return order ^ lax.axis_index(axis) if size == 4 else order


def split_slots(value, size):
    step = value.shape[0] // size
    return [value[i * step : (i + 1) * step] for i in range(size)]


def shards(
    sizes,
    layer_in,
    doc_ids,
    out_grad,
    query_weight,
    query_bias,
    key_weight,
    value_weight,
    value_bias,
    output_weight,
    output_bias,
    first_gain,
    first_shift,
    up_weight,
    up_bias,
    down_weight,
    down_bias,
    second_gain,
    second_shift,
):
    S, Z, C = sizes["seq"], sizes["z"], sizes["c"]
    devices = S * Z * C
    s, z, c = (lax.axis_index(a) for a in ALL)
    rows = query_weight.shape[0]
    hidden_units = up_weight.shape[1]
    share = hidden_units // devices
    slice_width = hidden_units // Z
    heads = H // Z
    tokens = layer_in.shape[2]
    whole_heads = rows * C == DH and H == S * Z
    cross = lambda value: swap(value, "c", C, 1)
    pick = lambda value, axis, i: lax.dynamic_index_in_dim(value, i, axis, keepdims=False)

    def place(value, axis, size, i):
        shape = list(value.shape)
        shape.insert(axis, size)
        start = [0] * len(shape)
        start[axis] = i
        return lax.dynamic_update_slice(
            jnp.zeros(shape, value.dtype), jnp.expand_dims(value, axis), start
        )

    def to_core(value):
        return jnp.concatenate([pick(value, 0, c)[0], cross(pick(value, 0, 1 - c)[0])], axis=0)

    def from_core(value):
        keep, came = value[:tokens], cross(value[tokens:])
        first = jnp.where(c == 0, keep, came)
        second = jnp.where(c == 0, came, keep)
        return jnp.stack([first, second])[:, None]

    def gather_rows(local):
        whole = lax.all_gather(
            local.reshape(-1, local.shape[2]), ("seq", "c"), axis=0, tiled=False
        )
        return whole.reshape(S, C, *local.shape).transpose(0, 2, 1, 3, 4)

    def by_owner(term):
        return term.reshape(S, Z, C, rows, -1).transpose(0, 2, 1, 3, 4).reshape(D, -1)

    width = 3 * heads * DH
    qkv_local = jnp.stack(
        [query_weight.astype(low), key_weight.astype(low), value_weight.astype(low)], axis=1
    )
    qkv_local = qkv_local.reshape(rows, 3, heads, Z, DH).transpose(3, 0, 1, 2, 4)
    own_vectors = [query_bias, value_bias, output_bias, first_gain, first_shift]
    own_vectors += [down_bias, second_gain, second_shift, up_bias]
    own_vectors = jnp.concatenate([v.astype(low) for v in own_vectors])
    extra = jnp.pad(own_vectors[None], ((0, 7), (0, width - own_vectors.shape[0])))
    qkv_local = jnp.concatenate(
        [qkv_local.reshape(Z, rows, width), jnp.broadcast_to(extra, (Z, 8, width))], axis=1
    )
    rounded_in, qkv_local = together(to_core(layer_in.astype(low)), qkv_local)
    gathered = gather_rows(exchange(qkv_local, "z", Z))
    if Z == 4:
        x_blocks, gathered = together(spread_2(*spread_1(rounded_in)), gathered)
        x_slots = spread_3(*x_blocks)
    else:
        x_slots = gather_slots(rounded_in, "z", Z)
    qkv_matrix = gathered[:, :, :, :rows].reshape(D, width)
    vectors = gathered[:, :, :, rows].reshape(devices, width)[:, : own_vectors.shape[0]]
    vectors = vectors.astype(wide)

    square = Z == 4 and S == 4 and whole_heads
    output_whole = lax.all_gather(output_weight.astype(low), ALL, axis=0, tiled=True)
    output_whole = output_whole.reshape(heads, Z, DH, D)
    output_matrix = pick(output_whole, 1, z).reshape(heads * DH, D)
    down_local = down_weight.astype(low)

    up_local = up_weight.astype(low).reshape(rows, S, Z, C * share).transpose(2, 0, 1, 3)
    up_local = up_local.reshape(Z, rows, slice_width)
    x_slots, up_local, layer_in, out_grad, qkv_matrix, vectors = together(
        x_slots, up_local, layer_in, out_grad, qkv_matrix, vectors
    )
    inputs, grad_output = to_core(layer_in), to_core(out_grad)
    if square:
        down_local, x_last = together(down_local, x_slots[-1])
        x_slots = [*x_slots[:-1], x_last]
        down_slots = gather_slots(down_local, "seq", S)
        down_matrix = jnp.zeros((S * C, share, D), low)
        for k, block in enumerate(down_slots):
            for i, value in enumerate((block, cross(block))):
                down_matrix = lax.dynamic_update_slice_in_dim(
                    down_matrix, value[None], (s * C + c) ^ (k * C + i), 0
                )
        down_matrix = down_matrix.reshape(slice_width, D)
    else:
        down_matrix = lax.all_gather(down_local, ("seq", "c"), axis=0, tiled=True)
    up_came = trade(up_local, "z", Z)

    vector = lambda i: vectors[:, i * rows : (i + 1) * rows].reshape(D)
    query_offset, value_offset = (
        pick(vector(i).reshape(heads, Z, DH), 1, z).reshape(heads * DH) for i in range(2)
    )
    (
        output_offset,
        first_scale,
        first_offset,
        down_offset,
        second_scale,
        second_offset,
    ) = (vector(i) for i in range(2, 8))
    up_offset = vectors[:, 8 * rows :].reshape(S, Z, C, share)
    up_offset = pick(up_offset, 1, z).reshape(slice_width)
    qkv_offset = jnp.concatenate([query_offset, jnp.zeros((heads * DH,), wide), value_offset])

    ids = pick(doc_ids, 0, c)[0].reshape(Z, C, tokens)
    ids = jnp.where(c == 0, ids, ids[:, ::-1])
    ids = ids[slot_order("z", Z)].reshape(-1)
    row_ids, col_ids = ids[:, None], ids[None, :]

    x_all = jnp.concatenate(x_slots, axis=0)
    qkv = (matmul(x_all, qkv_matrix) + qkv_offset).astype(low)
    mixed, totals = attend(qkv, row_ids, col_ids, heads)
    up_came, mixed = together(up_came, mixed)
    up_matrix = gather_rows(ordered(up_came, "z")).reshape(D, slice_width)
    if square:
        slot_weights = [pick(output_whole, 1, z ^ k).reshape(heads * DH, D) for k in range(Z)]
        h_all, hidden, first_normed, first_inverse = branch_norm(
            gather_slots(mixed, "z", Z),
            jnp.stack(slot_weights),
            x_all,
            inputs,
            jnp.stack([output_offset, first_scale, first_offset]),
        )
        h_slots = split_slots(h_all, Z)
    else:
        branch_parts = split_slots(matmul(mixed, output_matrix).astype(low), Z)
        branch = scatter_slots(branch_parts, "z", Z) + output_offset
        hidden, first_normed, first_inverse = normalize_forward(
            inputs + branch, first_scale, first_offset
        )
        h_slots = gather_slots(hidden.astype(low), "z", Z)

    def forward(h_slot):
        active, slope = gelu_both(matmul(h_slot, up_matrix) + up_offset)
        active = active.astype(low)
        return active, slope, lax.optimization_barrier(matmul(active, down_matrix).astype(low))

    done = [forward(h_slot) for h_slot in h_slots]
    actives, slopes, downs = zip(*done, strict=True)
    down = scatter_slots(downs, "z", Z) + down_offset
    result, second_normed, second_inverse = normalize_forward(
        hidden + down, second_scale, second_offset
    )

    grad_second, second_gain_part, second_shift_part = normalize_backward(
        grad_output, second_normed, second_inverse, second_scale
    )
    grad_down = grad_second.astype(low)
    g_slots = gather_slots(grad_down, "z", Z)
    grad_ups, hidden_parts = [], []
    for g_slot, slope in zip(g_slots, slopes, strict=True):
        grad_up = (against(g_slot, down_matrix) * slope).astype(low)
        grad_ups.append(grad_up)
        hidden_parts.append(lax.optimization_barrier(against(grad_up, up_matrix).astype(low)))

    joined = lambda values: jnp.concatenate(values, axis=0)
    grad_up_all = joined(grad_ups)
    down_term = transposed(joined(actives), joined(g_slots)).astype(low)
    up_term = transposed(joined(h_slots), grad_up_all).astype(low)
    if Z == 4:
        hidden_parts, down_term = together(sum_1(*hidden_parts), down_term)
        hidden_sum = sum_2(*hidden_parts)
    else:
        hidden_sum = scatter_slots(hidden_parts, "z", Z)
    down_mine = lax.psum_scatter(down_term, ("seq", "c"), scatter_dimension=0, tiled=True)
    grad_hidden = grad_second + hidden_sum

    grad_first, first_gain_part, first_shift_part = normalize_backward(
        grad_hidden, first_normed, first_inverse, first_scale
    )
    grad_branch = grad_first.astype(low)
    terms = [
        column_sum(grad_branch),
        first_gain_part,
        first_shift_part,
        column_sum(grad_down),
        second_gain_part,
        second_shift_part,
    ]
    terms = jnp.concatenate([v.reshape(devices, rows) for v in terms], axis=1).astype(low)
    below = -(-terms.size // D // 8) * 8
    terms = jnp.pad(terms.reshape(-1), (0, below * D - terms.size)).reshape(below, D)
    sent = jnp.concatenate([grad_branch, terms], axis=0)
    if Z == 4:
        b_blocks, up_term = together(spread_1(sent), by_owner(up_term))
        b_blocks, layer_out = together(spread_2(*b_blocks), from_core(result))
        b_slots = spread_3(*b_blocks)
    else:
        b_slots, up_term = gather_slots(sent, "z", Z), by_owner(up_term)
        layer_out = from_core(result)
    up_mine = lax.psum_scatter(up_term, ("seq", "c"), scatter_dimension=0, tiled=True)
    b_all = joined([v[:-below] for v in b_slots])
    term_sums = sum(v[-below:].astype(wide) for v in b_slots)
    term_sums = term_sums.reshape(-1)[: 6 * D].reshape(S, Z, C, 6 * rows)
    term_sums = pick(term_sums, 1, z)
    grad_mixed = against(b_all, output_matrix).astype(low)
    grad_query, grad_key, grad_value = attend_back(
        qkv, grad_mixed, totals, row_ids, col_ids, heads
    )
    grad_qkv = jnp.concatenate([grad_query, grad_key, grad_value], axis=1)
    in_parts = split_slots(against(grad_qkv, qkv_matrix).astype(low), Z)
    in_parts, grad_qkv_late, mixed_late, down_mine, term_sums = together(
        in_parts, grad_qkv, mixed, down_mine, term_sums
    )
    if Z == 4:
        in_parts, up_mine = together(sum_1(*in_parts), up_mine)
        in_sum = sum_2(*in_parts)
    else:
        in_sum = scatter_slots(in_parts, "z", Z)
    input_grad = from_core(grad_first + in_sum)
    down_weight_grad = down_mine.astype(wide)
    up_came = trade(up_mine.reshape(Z, rows, slice_width), "z", Z)

    def in_plane(term, rest):
        term = term.reshape(S, -1, C, rows, rest)
        both = add(pick(term, 2, c), cross(pick(term, 2, 1 - c))).reshape(S, -1, rest)
        parts = [both[i] for i in range(S)] if S != 4 else [pick(both, 0, s ^ k) for k in range(S)]
        return scatter_slots(parts, "seq", S)

    output_term = transposed(mixed_late, b_all).astype(low)
    if whole_heads:
        output_weight_grad = in_plane(output_term, D)
    else:
        output_term = place(output_term.reshape(heads, DH, D), 1, Z, z)
        output_weight_grad = lax.psum_scatter(
            output_term.reshape(D, D), ALL, scatter_dimension=0, tiled=True
        ).astype(wide)
    qkv_mine = in_plane(transposed(x_all, grad_qkv_late).astype(low), width).astype(low)
    qkv_came = trade(qkv_mine.reshape(Z, rows, width), "z", Z)
    up_came, qkv_came = together(up_came, qkv_came)
    up_mine = ordered(up_came, "z").reshape(Z, rows, S, C * share)
    up_weight_grad = up_mine.transpose(1, 2, 0, 3).reshape(rows, hidden_units).astype(wide)
    qkv_grads = ordered(qkv_came, "z").reshape(Z, rows, 3, heads, DH).transpose(2, 1, 3, 0, 4)
    qkv_grads = qkv_grads.reshape(3, rows, D).astype(wide)

    sums = sum_over(term_sums, ("c", "seq"), sizes)
    sums = pick(pick(sums, 0, s), 0, c)
    vec = lambda i: sums[i * rows : (i + 1) * rows]
    up_bias_grad = sum_over(column_sum(grad_up_all).reshape(S, C, share), ("c", "seq"), sizes)
    up_bias_grad = pick(pick(up_bias_grad, 0, s), 0, c)
    biases = column_sum(grad_qkv_late).reshape(3, heads * DH)
    biases = jnp.stack([biases[0], biases[2]])
    biases = sum_over(biases, ("c", "seq"), sizes)
    if whole_heads:
        biases = pick(pick(biases.reshape(2, S, C, rows), 1, s), 1, c)
    else:
        biases = lax.all_gather(biases.reshape(2, heads, DH), "z", axis=2, tiled=False)
        biases = pick(biases.reshape(2, devices, rows), 1, (s * Z + z) * C + c)
    return (
        layer_out,
        input_grad,
        qkv_grads[0],
        biases[0],
        qkv_grads[1],
        qkv_grads[2],
        biases[1],
        output_weight_grad,
        vec(0),
        vec(1),
        vec(2),
        up_weight_grad,
        up_bias_grad,
        down_weight_grad,
        vec(3),
        vec(4),
        vec(5),
    )


def solution(mesh):
    sizes = {"seq": mesh.shape["seq"], "z": mesh.shape["fsdp"] // CORES, "c": CORES}
    inner = Mesh(mesh.devices.reshape(tuple(sizes[a] for a in ALL)), ALL)
    token = P(None, "seq", ("z", "c"), None)
    matrix = P(ALL, None)
    vector = P(ALL)
    return jax.shard_map(
        functools.partial(shards, sizes),
        mesh=inner,
        in_specs=(
            token,
            P(None, "seq", None),
            token,
            matrix,
            vector,
            matrix,
            matrix,
            vector,
            matrix,
            vector,
            vector,
            vector,
            matrix,
            vector,
            matrix,
            vector,
            vector,
            vector,
        ),
        out_specs=(
            token,
            token,
            matrix,
            vector,
            matrix,
            matrix,
            vector,
            matrix,
            vector,
            vector,
            vector,
            matrix,
            vector,
            matrix,
            vector,
            vector,
            vector,
        ),
        check_vma=False,
    )
```

```python
import functools

import jax
import jax.numpy as jnp
from jax import lax
from jax.experimental import pallas as pl
from jax.experimental.pallas import tpu as pltpu
from jax.sharding import Mesh
from jax.sharding import PartitionSpec as P

D = 2048
H = 16
DH = 128
MB = 2
CORES = 2

low = jnp.bfloat16
wide = jnp.float32
norm_eps = 1e-06
masked_score = -1e30
score_scale = DH ** (-0.5)
ALL = ("seq", "z", "c")


def normalize_forward(summed, gain_vector, shift_vector):
    center = summed - jnp.mean(summed, axis=-1, keepdims=True)
    inverse = lax.rsqrt(jnp.mean(center * center, axis=-1, keepdims=True) + norm_eps)
    normed = center * inverse
    return (normed * gain_vector + shift_vector, normed, inverse)


def normalize_backward(grad_output, normed, inverse, gain_vector):
    grad_normed = grad_output * gain_vector
    centered = grad_normed - jnp.mean(grad_normed, axis=-1, keepdims=True)
    grad_input = inverse * (
        centered - normed * jnp.mean(grad_normed * normed, axis=-1, keepdims=True)
    )
    return (grad_input, jnp.sum(grad_output * normed, axis=0), jnp.sum(grad_output, axis=0))


def matmul(left, right):
    return jnp.dot(left, right, preferred_element_type=wide)


def transposed(left, right):
    return jnp.einsum("ti,tj->ij", left, right, preferred_element_type=wide)


def against(left, right):
    return jnp.einsum("ti,ji->tj", left, right, preferred_element_type=wide)


def column_sum(matrix):
    return jnp.sum(matrix.astype(wide), axis=0)


def gelu_both(u):
    root = (2.0 / jnp.pi) ** 0.5
    cubic = 0.044715
    square = u * u
    bend = jnp.tanh(root * (u + cubic * u * square))
    half = 0.5 * (1.0 + bend)
    slope = half + 0.5 * u * (1.0 - bend * bend) * (root * (1.0 + 3.0 * cubic * square))
    return u * half, slope


def nt(left, right):
    return lax.dot_general(left, right, (((1,), (1,)), ((), ())), preferred_element_type=wide)


def tn(left, right):
    return lax.dot_general(left, right, (((0,), (0,)), ((), ())), preferred_element_type=wide)


def attend_kernel(rows, q_ref, k_ref, v_ref, row_ref, col_ref, o_ref, total_ref):
    keys = k_ref[...]
    values = v_ref[...]
    cols = col_ref[...]
    for start in range(0, q_ref.shape[0], rows):
        here = pl.ds(start, rows)
        scores = nt(q_ref[here, :], keys) * score_scale
        scores = jnp.where(row_ref[here, :] == cols, scores, masked_score)
        top = jnp.max(scores, axis=-1, keepdims=True)
        raised = jnp.exp(scores - top)
        total = jnp.sum(raised, axis=-1, keepdims=True)
        probs = (raised * (1.0 / total)).astype(low)
        o_ref[here, :] = jnp.dot(probs, values, preferred_element_type=wide).astype(low)
        total_ref[0, here, :] = top + jnp.log(total)


def attend_back_kernel(
    rows, q_ref, k_ref, v_ref, g_ref, total_ref, row_ref, col_ref, dq_ref, dk_ref, dv_ref, ka, va
):
    keys = k_ref[...]
    values = v_ref[...]
    cols = col_ref[...]
    for start in range(0, q_ref.shape[0], rows):
        here = pl.ds(start, rows)
        queries = q_ref[here, :]
        grads = g_ref[here, :]
        scores = nt(queries, keys) * score_scale
        scores = jnp.where(row_ref[here, :] == cols, scores, masked_score)
        probs = jnp.exp(scores - total_ref[0, here, :])
        grad_probs = nt(grads, values)
        row_dot = jnp.sum(probs * grad_probs, axis=-1, keepdims=True)
        grad_scores = (probs * (grad_probs - row_dot)).astype(low)
        dq_ref[here, :] = (
            jnp.dot(grad_scores, keys, preferred_element_type=wide) * score_scale
        ).astype(low)
        dk_part = tn(grad_scores, queries)
        dv_part = tn(probs.astype(low), grads)
        if start == 0:
            ka[...] = dk_part
            va[...] = dv_part
        else:
            ka[...] += dk_part
            va[...] += dv_part
    dk_ref[...] = (ka[...] * score_scale).astype(low)
    dv_ref[...] = va[...].astype(low)


def attend(qkv, row_ids, col_ids, heads):
    length = qkv.shape[0]
    rows = min(256, length)
    block = lambda part: pl.BlockSpec((length, DH), lambda h: (0, part * heads + h))
    return pl.pallas_call(
        functools.partial(attend_kernel, rows),
        grid=(heads,),
        in_specs=[
            block(0),
            block(1),
            block(2),
            pl.BlockSpec((length, 1), lambda h: (0, 0)),
            pl.BlockSpec((1, length), lambda h: (0, 0)),
        ],
        out_specs=[
            pl.BlockSpec((length, DH), lambda h: (0, h)),
            pl.BlockSpec((1, length, 1), lambda h: (h, 0, 0)),
        ],
        out_shape=[
            jax.ShapeDtypeStruct((length, heads * DH), low),
            jax.ShapeDtypeStruct((heads, length, 1), wide),
        ],
        cost_estimate=pl.CostEstimate(
            flops=4 * heads * length * length * DH,
            bytes_accessed=8 * heads * length * DH,
            transcendentals=heads * length * length,
        ),
        compiler_params=pltpu.CompilerParams(vmem_limit_bytes=40 * 2**20),
        name="attend",
    )(qkv, qkv, qkv, row_ids, col_ids)


def attend_back(qkv, grad_mixed, totals, row_ids, col_ids, heads):
    length = qkv.shape[0]
    rows = min(256, length)
    block = lambda part: pl.BlockSpec((length, DH), lambda h: (0, part * heads + h))
    out = pl.BlockSpec((length, DH), lambda h: (0, h))
    shape = jax.ShapeDtypeStruct((length, heads * DH), low)
    return pl.pallas_call(
        functools.partial(attend_back_kernel, rows),
        grid=(heads,),
        in_specs=[
            block(0),
            block(1),
            block(2),
            out,
            pl.BlockSpec((1, length, 1), lambda h: (h, 0, 0)),
            pl.BlockSpec((length, 1), lambda h: (0, 0)),
            pl.BlockSpec((1, length), lambda h: (0, 0)),
        ],
        out_specs=[out, out, out],
        out_shape=[shape, shape, shape],
        scratch_shapes=[pltpu.VMEM((length, DH), wide), pltpu.VMEM((length, DH), wide)],
        cost_estimate=pl.CostEstimate(
            flops=10 * heads * length * length * DH,
            bytes_accessed=16 * heads * length * DH,
            transcendentals=heads * length * length,
        ),
        compiler_params=pltpu.CompilerParams(vmem_limit_bytes=48 * 2**20),
        name="attend_back",
    )(qkv, qkv, qkv, grad_mixed, totals, row_ids, col_ids)


def branch_kernel(*refs):
    *mixed_refs, w_ref, x_ref, own_ref, vector_ref = refs[:-4]
    low_ref, hidden_ref, normed_ref, inverse_ref = refs[-4:]
    branch = vector_ref[0:1, :]
    for k, mixed_ref in enumerate(mixed_refs):
        branch = branch + jnp.dot(mixed_ref[...], w_ref[k], preferred_element_type=wide)
    here = pl.program_id(0) == 0
    tokens = jnp.where(here, own_ref[...], x_ref[...].astype(wide))
    hidden, normed, inverse = normalize_forward(
        tokens + branch, vector_ref[1:2, :], vector_ref[2:3, :]
    )
    low_ref[...] = hidden.astype(low)

    @pl.when(here)
    def _():
        hidden_ref[...] = hidden
        normed_ref[...] = normed
        inverse_ref[...] = inverse


def branch_norm(mixed_slots, weights, x_all, own, vectors):
    size = len(mixed_slots)
    block, width = own.shape
    fed = mixed_slots[0].shape[1]
    row = pl.BlockSpec((block, width), lambda i: (i, 0))
    kept = pl.BlockSpec((block, width), lambda i: (0, 0))
    specs = [pl.BlockSpec((block, fed), lambda i, k=k: (i ^ k, 0)) for k in range(size)]
    return pl.pallas_call(
        branch_kernel,
        grid=(size,),
        in_specs=[
            *specs,
            pl.BlockSpec((size, fed, width), lambda i: (0, 0, 0)),
            row,
            kept,
            pl.BlockSpec(vectors.shape, lambda i: (0, 0)),
        ],
        out_specs=[row, kept, kept, pl.BlockSpec((block, 1), lambda i: (0, 0))],
        out_shape=[
            jax.ShapeDtypeStruct((size * block, width), low),
            jax.ShapeDtypeStruct((block, width), wide),
            jax.ShapeDtypeStruct((block, width), wide),
            jax.ShapeDtypeStruct((block, 1), wide),
        ],
        cost_estimate=pl.CostEstimate(
            flops=2 * size * block * size * fed * width,
            bytes_accessed=2 * size * fed * width + 16 * size * block * width,
            transcendentals=size * block,
        ),
        compiler_params=pltpu.CompilerParams(vmem_limit_bytes=52 * 2**20),
        name="branch_norm",
    )(*mixed_slots, weights, x_all, own, vectors)


def swap(value, axis, size, bit):
    return lax.ppermute(value, axis, [(i, i ^ bit) for i in range(size)])


def together(*values):
    return lax.optimization_barrier(values)


def trade(value, axis, size):
    here = lax.axis_index(axis)
    pick = lambda i: lax.dynamic_index_in_dim(value, i, 0, keepdims=False)
    return [pick(here)] + [swap(pick(here ^ k), axis, size, k) for k in range(1, size)]


def ordered(came, axis):
    here = lax.axis_index(axis)
    size = len(came)
    return jnp.stack([lax.select_n(here, *(came[i ^ k] for k in range(size))) for i in range(size)])


def exchange(value, axis, size):
    return ordered(trade(value, axis, size), axis)


def bits(size):
    step = 1
    while step < size:
        yield step
        step *= 2


def sum_over(value, axes, sizes):
    for axis in axes:
        for bit in bits(sizes[axis]):
            value = value + swap(value, axis, sizes[axis], bit)
    return value


ENDS = [(0, 1), (1, 0), (2, 3), (3, 2)]
MIDDLE = [(1, 2), (2, 1)]
OUTWARD = [(1, 0), (2, 3)]
INWARD = [(0, 1), (3, 2)]


def send(value, pairs):
    return lax.ppermute(value, "z", pairs)


def add(left, right):
    return (left.astype(wide) + right.astype(wide)).astype(low)


def spread_1(own):
    return own, send(own, ENDS), send(own, MIDDLE)


def spread_2(own, first, third):
    return own, first, send(first, MIDDLE), send(third, OUTWARD), third


def spread_3(own, first, second_in, second_out, third_in):
    inner = (lax.axis_index("z") == 1) | (lax.axis_index("z") == 2)
    third_out = send(second_in, OUTWARD)
    return [
        own,
        first,
        jnp.where(inner, second_in, second_out),
        jnp.where(inner, third_in, third_out),
    ]


def sum_1(own, first, second, third):
    second_came = send(second, INWARD)
    first_came = send(add(second, send(third, INWARD)), MIDDLE)
    second_came, first_came = together(second_came, first_came)
    return own, add(first, first_came), add(third, second_came)


def sum_2(own, first, third):
    from_end, from_middle = send(first, ENDS), send(third, MIDDLE)
    return own.astype(wide) + from_middle.astype(wide) + from_end.astype(wide)


def gather_slots(own, axis, size):
    if size != 4:
        whole = lax.all_gather(own, axis, axis=0)
        return [whole[i] for i in range(size)]
    if axis == "z":
        return spread_3(*spread_2(*spread_1(own)))
    half = own.shape[0] // 2
    first = swap(own, axis, 4, 1)
    second = swap(own, axis, 4, 2)
    third_top = swap(first[:half], axis, 4, 2)
    third_end = swap(second[half:], axis, 4, 1)
    return [own, first, second, jnp.concatenate([third_top, third_end], axis=0)]


def scatter_slots(parts, axis, size):
    if size != 4:
        return lax.psum_scatter(jnp.stack(parts), axis, scatter_dimension=0, tiled=False).astype(
            wide
        )
    if axis == "z":
        return sum_2(*sum_1(*parts))
    own, first, second, third = parts
    half = own.shape[0] // 2
    top = swap(third[:half], axis, 4, 2)
    end = swap(third[half:], axis, 4, 1)
    first_full = jnp.concatenate([add(first[:half], top), first[half:]], axis=0)
    second_full = jnp.concatenate([second[:half], add(second[half:], end)], axis=0)
    from_first = swap(first_full, axis, 4, 1)
    from_second = swap(second_full, axis, 4, 2)
    return own.astype(wide) + from_first.astype(wide) + from_second.astype(wide)


def slot_order(axis, size):
    order = jnp.arange(size)
    return order ^ lax.axis_index(axis) if size == 4 else order


def split_slots(value, size):
    step = value.shape[0] // size
    return [value[i * step : (i + 1) * step] for i in range(size)]


def shards(
    sizes,
    layer_in,
    doc_ids,
    out_grad,
    query_weight,
    query_bias,
    key_weight,
    value_weight,
    value_bias,
    output_weight,
    output_bias,
    first_gain,
    first_shift,
    up_weight,
    up_bias,
    down_weight,
    down_bias,
    second_gain,
    second_shift,
):
    S, Z, C = sizes["seq"], sizes["z"], sizes["c"]
    devices = S * Z * C
    s, z, c = (lax.axis_index(a) for a in ALL)
    rows = query_weight.shape[0]
    hidden_units = up_weight.shape[1]
    share = hidden_units // devices
    slice_width = hidden_units // Z
    heads = H // Z
    tokens = layer_in.shape[2]
    whole_heads = rows * C == DH and H == S * Z
    cross = lambda value: swap(value, "c", C, 1)
    pick = lambda value, axis, i: lax.dynamic_index_in_dim(value, i, axis, keepdims=False)

    def place(value, axis, size, i):
        shape = list(value.shape)
        shape.insert(axis, size)
        start = [0] * len(shape)
        start[axis] = i
        return lax.dynamic_update_slice(
            jnp.zeros(shape, value.dtype), jnp.expand_dims(value, axis), start
        )

    def to_core(value):
        return jnp.concatenate([pick(value, 0, c)[0], cross(pick(value, 0, 1 - c)[0])], axis=0)

    def from_core(value):
        keep, came = value[:tokens], cross(value[tokens:])
        first = jnp.where(c == 0, keep, came)
        second = jnp.where(c == 0, came, keep)
        return jnp.stack([first, second])[:, None]

    def gather_rows(local):
        whole = lax.all_gather(
            local.reshape(-1, local.shape[2]), ("seq", "c"), axis=0, tiled=False
        )
        return whole.reshape(S, C, *local.shape).transpose(0, 2, 1, 3, 4)

    def by_owner(term):
        return term.reshape(S, Z, C, rows, -1).transpose(0, 2, 1, 3, 4).reshape(D, -1)

    width = 3 * heads * DH
    qkv_local = jnp.stack(
        [query_weight.astype(low), key_weight.astype(low), value_weight.astype(low)], axis=1
    )
    qkv_local = qkv_local.reshape(rows, 3, heads, Z, DH).transpose(3, 0, 1, 2, 4)
    own_vectors = [query_bias, value_bias, output_bias, first_gain, first_shift]
    own_vectors += [down_bias, second_gain, second_shift, up_bias]
    own_vectors = jnp.concatenate([v.astype(low) for v in own_vectors])
    extra = jnp.pad(own_vectors[None], ((0, 7), (0, width - own_vectors.shape[0])))
    qkv_local = jnp.concatenate(
        [qkv_local.reshape(Z, rows, width), jnp.broadcast_to(extra, (Z, 8, width))], axis=1
    )
    rounded_in, qkv_local = together(to_core(layer_in.astype(low)), qkv_local)
    gathered = gather_rows(exchange(qkv_local, "z", Z))
    if Z == 4:
        x_blocks, gathered = together(spread_2(*spread_1(rounded_in)), gathered)
        x_slots = spread_3(*x_blocks)
    else:
        x_slots = gather_slots(rounded_in, "z", Z)
    qkv_matrix = gathered[:, :, :, :rows].reshape(D, width)
    vectors = gathered[:, :, :, rows].reshape(devices, width)[:, : own_vectors.shape[0]]
    vectors = vectors.astype(wide)

    square = Z == 4 and S == 4 and whole_heads
    if square:
        output_slots = jnp.concatenate(gather_slots(output_weight.astype(low), "z", Z), axis=0)
        output_whole = lax.all_gather(output_slots, ("seq", "c"), axis=0, tiled=False)
        output_whole = output_whole.reshape(S * C, Z, rows, D).transpose(1, 0, 2, 3)
        output_whole = output_whole.reshape(Z, heads * DH, D)
        output_matrix = output_whole[0]
    else:
        output_whole = lax.all_gather(output_weight.astype(low), ALL, axis=0, tiled=True)
        output_matrix = pick(output_whole.reshape(heads, Z, DH, D), 1, z).reshape(heads * DH, D)
    down_local = down_weight.astype(low)

    up_local = up_weight.astype(low).reshape(rows, S, Z, C * share).transpose(2, 0, 1, 3)
    up_local = up_local.reshape(Z, rows, slice_width)
    x_slots, up_local, layer_in, out_grad, qkv_matrix, vectors = together(
        x_slots, up_local, layer_in, out_grad, qkv_matrix, vectors
    )
    inputs, grad_output = to_core(layer_in), to_core(out_grad)
    if square:
        down_local, x_last = together(down_local, x_slots[-1])
        x_slots = [*x_slots[:-1], x_last]
        down_slots = gather_slots(down_local, "seq", S)
        down_matrix = jnp.zeros((S * C, share, D), low)
        for k, block in enumerate(down_slots):
            for i, value in enumerate((block, cross(block))):
                down_matrix = lax.dynamic_update_slice_in_dim(
                    down_matrix, value[None], (s * C + c) ^ (k * C + i), 0
                )
        down_matrix = down_matrix.reshape(slice_width, D)
    else:
        down_matrix = lax.all_gather(down_local, ("seq", "c"), axis=0, tiled=True)
    up_came = trade(up_local, "z", Z)

    vector = lambda i: vectors[:, i * rows : (i + 1) * rows].reshape(D)
    query_offset, value_offset = (
        pick(vector(i).reshape(heads, Z, DH), 1, z).reshape(heads * DH) for i in range(2)
    )
    (
        output_offset,
        first_scale,
        first_offset,
        down_offset,
        second_scale,
        second_offset,
    ) = (vector(i) for i in range(2, 8))
    up_offset = vectors[:, 8 * rows :].reshape(S, Z, C, share)
    up_offset = pick(up_offset, 1, z).reshape(slice_width)
    qkv_offset = jnp.concatenate([query_offset, jnp.zeros((heads * DH,), wide), value_offset])

    ids = pick(doc_ids, 0, c)[0].reshape(Z, C, tokens)
    ids = jnp.where(c == 0, ids, ids[:, ::-1])
    ids = ids[slot_order("z", Z)].reshape(-1)
    row_ids, col_ids = ids[:, None], ids[None, :]

    x_all = jnp.concatenate(x_slots, axis=0)
    qkv = (matmul(x_all, qkv_matrix) + qkv_offset).astype(low)
    mixed, totals = attend(qkv, row_ids, col_ids, heads)
    up_came, mixed = together(up_came, mixed)
    up_matrix = gather_rows(ordered(up_came, "z")).reshape(D, slice_width)
    if square:
        h_all, hidden, first_normed, first_inverse = branch_norm(
            gather_slots(mixed, "z", Z),
            output_whole,
            x_all,
            inputs,
            jnp.stack([output_offset, first_scale, first_offset]),
        )
        h_slots = split_slots(h_all, Z)
    else:
        branch_parts = split_slots(matmul(mixed, output_matrix).astype(low), Z)
        branch = scatter_slots(branch_parts, "z", Z) + output_offset
        hidden, first_normed, first_inverse = normalize_forward(
            inputs + branch, first_scale, first_offset
        )
        h_slots = gather_slots(hidden.astype(low), "z", Z)

    def forward(h_slot):
        active, slope = gelu_both(matmul(h_slot, up_matrix) + up_offset)
        active = active.astype(low)
        return active, slope, lax.optimization_barrier(matmul(active, down_matrix).astype(low))

    done = [forward(h_slot) for h_slot in h_slots]
    actives, slopes, downs = zip(*done, strict=True)
    down = scatter_slots(downs, "z", Z) + down_offset
    result, second_normed, second_inverse = normalize_forward(
        hidden + down, second_scale, second_offset
    )

    grad_second, second_gain_part, second_shift_part = normalize_backward(
        grad_output, second_normed, second_inverse, second_scale
    )
    grad_down = grad_second.astype(low)
    g_slots = gather_slots(grad_down, "z", Z)
    grad_ups, hidden_parts = [], []
    for g_slot, slope in zip(g_slots, slopes, strict=True):
        grad_up = (against(g_slot, down_matrix) * slope).astype(low)
        grad_ups.append(grad_up)
        hidden_parts.append(lax.optimization_barrier(against(grad_up, up_matrix).astype(low)))

    joined = lambda values: jnp.concatenate(values, axis=0)
    grad_up_all = joined(grad_ups)
    down_term = transposed(joined(actives), joined(g_slots)).astype(low)
    up_term = transposed(joined(h_slots), grad_up_all).astype(low)
    if Z == 4:
        hidden_parts, down_term = together(sum_1(*hidden_parts), down_term)
        hidden_sum = sum_2(*hidden_parts)
    else:
        hidden_sum = scatter_slots(hidden_parts, "z", Z)
    down_mine = lax.psum_scatter(down_term, ("seq", "c"), scatter_dimension=0, tiled=True)
    grad_hidden = grad_second + hidden_sum

    grad_first, first_gain_part, first_shift_part = normalize_backward(
        grad_hidden, first_normed, first_inverse, first_scale
    )
    grad_branch = grad_first.astype(low)
    terms = [
        column_sum(grad_branch),
        first_gain_part,
        first_shift_part,
        column_sum(grad_down),
        second_gain_part,
        second_shift_part,
    ]
    terms = jnp.concatenate([v.reshape(devices, rows) for v in terms], axis=1).astype(low)
    below = -(-terms.size // D // 8) * 8
    terms = jnp.pad(terms.reshape(-1), (0, below * D - terms.size)).reshape(below, D)
    sent = jnp.concatenate([grad_branch, terms], axis=0)
    if Z == 4:
        b_blocks, up_term = together(spread_1(sent), by_owner(up_term))
        b_blocks, layer_out = together(spread_2(*b_blocks), from_core(result))
        b_slots = spread_3(*b_blocks)
    else:
        b_slots, up_term = gather_slots(sent, "z", Z), by_owner(up_term)
        layer_out = from_core(result)
    up_mine = lax.psum_scatter(up_term, ("seq", "c"), scatter_dimension=0, tiled=True)
    b_all = joined([v[:-below] for v in b_slots])
    term_sums = sum(v[-below:].astype(wide) for v in b_slots)
    term_sums = term_sums.reshape(-1)[: 6 * D].reshape(S, Z, C, 6 * rows)
    term_sums = pick(term_sums, 1, z)
    grad_mixed = against(b_all, output_matrix).astype(low)
    grad_query, grad_key, grad_value = attend_back(
        qkv, grad_mixed, totals, row_ids, col_ids, heads
    )
    grad_qkv = jnp.concatenate([grad_query, grad_key, grad_value], axis=1)
    in_parts = split_slots(against(grad_qkv, qkv_matrix).astype(low), Z)
    in_parts, grad_qkv_late, mixed_late, down_mine, term_sums = together(
        in_parts, grad_qkv, mixed, down_mine, term_sums
    )
    if Z == 4:
        in_parts, up_mine = together(sum_1(*in_parts), up_mine)
        in_sum = sum_2(*in_parts)
    else:
        in_sum = scatter_slots(in_parts, "z", Z)
    input_grad = from_core(grad_first + in_sum)
    down_weight_grad = down_mine.astype(wide)
    up_came = trade(up_mine.reshape(Z, rows, slice_width), "z", Z)

    def in_plane(term, rest):
        term = term.reshape(S, -1, C, rows, rest)
        both = add(pick(term, 2, c), cross(pick(term, 2, 1 - c))).reshape(S, -1, rest)
        parts = [both[i] for i in range(S)] if S != 4 else [pick(both, 0, s ^ k) for k in range(S)]
        return scatter_slots(parts, "seq", S)

    output_term = transposed(mixed_late, b_all).astype(low)
    if whole_heads:
        output_weight_grad = in_plane(output_term, D)
    else:
        output_term = place(output_term.reshape(heads, DH, D), 1, Z, z)
        output_weight_grad = lax.psum_scatter(
            output_term.reshape(D, D), ALL, scatter_dimension=0, tiled=True
        ).astype(wide)
    qkv_mine = in_plane(transposed(x_all, grad_qkv_late).astype(low), width).astype(low)
    qkv_came = trade(qkv_mine.reshape(Z, rows, width), "z", Z)
    up_came, qkv_came = together(up_came, qkv_came)
    up_mine = ordered(up_came, "z").reshape(Z, rows, S, C * share)
    up_weight_grad = up_mine.transpose(1, 2, 0, 3).reshape(rows, hidden_units).astype(wide)
    qkv_grads = ordered(qkv_came, "z").reshape(Z, rows, 3, heads, DH).transpose(2, 1, 3, 0, 4)
    qkv_grads = qkv_grads.reshape(3, rows, D).astype(wide)

    sums = sum_over(term_sums, ("c", "seq"), sizes)
    sums = pick(pick(sums, 0, s), 0, c)
    vec = lambda i: sums[i * rows : (i + 1) * rows]
    up_bias_grad = sum_over(column_sum(grad_up_all).reshape(S, C, share), ("c", "seq"), sizes)
    up_bias_grad = pick(pick(up_bias_grad, 0, s), 0, c)
    biases = column_sum(grad_qkv_late).reshape(3, heads * DH)
    biases = jnp.stack([biases[0], biases[2]])
    biases = sum_over(biases, ("c", "seq"), sizes)
    if whole_heads:
        biases = pick(pick(biases.reshape(2, S, C, rows), 1, s), 1, c)
    else:
        biases = lax.all_gather(biases.reshape(2, heads, DH), "z", axis=2, tiled=False)
        biases = pick(biases.reshape(2, devices, rows), 1, (s * Z + z) * C + c)
    return (
        layer_out,
        input_grad,
        qkv_grads[0],
        biases[0],
        qkv_grads[1],
        qkv_grads[2],
        biases[1],
        output_weight_grad,
        vec(0),
        vec(1),
        vec(2),
        up_weight_grad,
        up_bias_grad,
        down_weight_grad,
        vec(3),
        vec(4),
        vec(5),
    )


def solution(mesh):
    sizes = {"seq": mesh.shape["seq"], "z": mesh.shape["fsdp"] // CORES, "c": CORES}
    inner = Mesh(mesh.devices.reshape(tuple(sizes[a] for a in ALL)), ALL)
    token = P(None, "seq", ("z", "c"), None)
    matrix = P(ALL, None)
    vector = P(ALL)
    return jax.shard_map(
        functools.partial(shards, sizes),
        mesh=inner,
        in_specs=(
            token,
            P(None, "seq", None),
            token,
            matrix,
            vector,
            matrix,
            matrix,
            vector,
            matrix,
            vector,
            vector,
            vector,
            matrix,
            vector,
            matrix,
            vector,
            vector,
            vector,
        ),
        out_specs=(
            token,
            token,
            matrix,
            vector,
            matrix,
            matrix,
            vector,
            matrix,
            vector,
            vector,
            vector,
            matrix,
            vector,
            matrix,
            vector,
            vector,
            vector,
        ),
        check_vma=False,
    )
```
